1024 devices in a mesh: boxes: 16 (over x, core), dirs: 64 (over y, z).
Axes of the slice: x: 8, y: 8, z: 8, core: 2. Of those that a mesh axis runs over, the one named last changes fastest.
Arguments:
- child_outgoing: float32 [8192, 2, 2048], P(('boxes', 'dirs')), may hold values from -6 to 6
- trans_table: float32 [316, 2, 8192], P(None, None, 'dirs'), may hold values from -0.4364358 to 0.4364358
- send_rows: int32 [16, 16, 32], replicated, may hold values from 0 to 63, as said below
- far_slot: int32 [1024, 189], P('boxes'), may hold values from 0 to 511
- far_trans: int32 [1024, 189], P('boxes'), may hold values from 0 to 315
- far_count: int32 [1024], P('boxes'), may hold values from 1 to 189, as said below
Outputs:
- child_incoming: float32 [8192, 2, 2048], P(('boxes', 'dirs'))
The draws below stay inside these ranges and needn't reach their ends.
Inputs may be any that keep to these rules, and one draw needn't show every extreme that they name: send_rows[g, h] lists 32 distinct parents of group g, as numbers within the group, whose outgoing fields group h reads. Slot g * 32 + q of far_slot names the parent send_rows[g, h, q] for a target of group h. Entries of a parent's far lists at positions far_count and beyond are unused; some parent has 189 live entries.
All inputs are finite; a program needn't handle non-finite values.
Results may differ from the reference program's by a relative error of at most 0.0003.
Values sent between devices are 32-bit elements; how exact they have to be, the bound alone decides.
A program may use at most 32 MiB of HBM per device.

```python
import math
import jax
import jax.numpy as jnp
from jax import lax

TC = 32
PC = 64
TP = 64
PP = 128
NTRANS = 316
NFAR = 189
KC = 2048
KP = 8192
PG = 64
CAP = 32
GROUPS = 16
PARENTS = 1024
CHILDREN = 8192


def draw_send_rows(key, part):
    keys = jax.random.split(jax.random.fold_in(key, 11), GROUPS * GROUPS)

    def one_pair(pair_key):
        return jax.random.permutation(pair_key, PG)[:CAP].astype(jnp.int32)
    chosen = jax.vmap(one_pair)(keys)
    return chosen.reshape(GROUPS, GROUPS, CAP).astype(jnp.int32)


def draw_far_count(key, part):
    base = jax.random.fold_in(key, 23)
    group_key, row_key, pick_key, top_key = jax.random.split(base, 4)
    halvings = jax.random.randint(group_key, (GROUPS,), 0, 4)
    ceilings = NFAR // 2 ** halvings
    busiest = jax.random.randint(top_key, (), 0, GROUPS)
    ceilings = jnp.where(jnp.arange(GROUPS) == busiest, NFAR, ceilings)
    per_row = jnp.repeat(ceilings, PG)
    counts = jax.random.randint(row_key, (PARENTS,), per_row // 8 + 1, per_row + 1)
    chosen = jax.random.randint(pick_key, (), 0, PG) + busiest * PG
    counts = jnp.where(jnp.arange(PARENTS) == chosen, NFAR, counts)
    return counts.astype(jnp.int32)


def set_ends(values, own_key, least, largest):
    spot = [jax.random.randint(jax.random.fold_in(own_key, axis), (), 0, length) for axis, length in enumerate(values.shape)]
    main_axis = values.shape.index(max(values.shape))
    beside = spot[:main_axis] + [(spot[main_axis] + 1) % values.shape[main_axis]] + spot[main_axis + 1:]
    return values.at[tuple(spot)].set(least).at[tuple(beside)].set(largest)


def shard_levels(own_key, dims, shards, low, top_value):
    factor_of = 1.0
    for axis_at, parts in shards:
        steps = jax.random.uniform(jax.random.fold_in(jax.random.fold_in(own_key, 6), axis_at), (parts,), jnp.float32, low / len(shards), top_value / len(shards))
        factor_of = factor_of * jnp.repeat(jnp.exp(steps), dims[axis_at] // parts).reshape((-1,) + (1,) * (len(dims) - 1 - axis_at))
    return factor_of


def normal_values(key, extent, width, reach, cuts=(), kind=jnp.bfloat16):
    entries = jax.random.normal(key, extent, jnp.float32) * width
    if len(cuts) > 0:
        entries = shard_levels(key, extent, cuts, -0.22, 0.18) * entries
    return jnp.clip(entries, min=-reach, max=reach).astype(kind)


def setup_inputs(seed: int = 0) -> dict:
    key_of = jax.random.split(jax.random.key(seed), 7)
    child_outgoing = normal_values(key_of[0], (CHILDREN, 2, KC), 1.0, 6.0, ((0, 1024),), jnp.float32)
    trans_table = normal_values(key_of[1], (NTRANS, 2, KP), (1.0 / NFAR ** 0.5), 0.4364358, ((2, 64),), jnp.float32)
    send_rows = draw_send_rows(jax.random.fold_in(key_of[6], 71), 0)
    far_slot = set_ends(jax.random.randint(key_of[3], (PARENTS, NFAR), 0, GROUPS * CAP), jax.random.fold_in(key_of[3], 1), 0, (GROUPS * CAP) - 1).astype(jnp.int32)
    far_trans = set_ends(jax.random.randint(key_of[4], (PARENTS, NFAR), 0, NTRANS), jax.random.fold_in(key_of[4], 1), 0, NTRANS - 1).astype(jnp.int32)
    far_count = draw_far_count(jax.random.fold_in(key_of[6], 71), 0)
    return dict(child_outgoing=child_outgoing, trans_table=trans_table, send_rows=send_rows, far_slot=far_slot, far_trans=far_trans, far_count=far_count)


shift_phase = 2.7


def interp_matrix(count_out, count_in, offset):
    target = (jnp.arange(count_out, dtype=jnp.float32) + offset) / count_out
    source = (jnp.arange(count_in, dtype=jnp.float32) + offset) / count_in
    spread = target[:, None] - source[None, :]
    orders = jnp.arange(1, count_in // 2, dtype=jnp.float32)
    series = jnp.sum(jnp.cos(2.0 * math.pi * orders[None, None, :] * spread[:, :, None]), axis=2)
    return (1.0 + 2.0 * series + jnp.cos(math.pi * count_in * spread)) / count_in


def phase_tables():
    polar = math.pi * (jnp.arange(TP, dtype=jnp.float32) + 0.5) / TP
    azimuth = 2.0 * math.pi * jnp.arange(PP, dtype=jnp.float32) / PP
    wave_x = jnp.sin(polar)[:, None] * jnp.cos(azimuth)[None, :]
    wave_y = jnp.sin(polar)[:, None] * jnp.sin(azimuth)[None, :]
    wave_z = jnp.cos(polar)[:, None] * jnp.ones((1, PP), jnp.float32)
    octant = jnp.arange(8, dtype=jnp.int32)
    sign_x = (2 * (octant % 2) - 1).astype(jnp.float32)[:, None, None]
    sign_y = (2 * ((octant // 2) % 2) - 1).astype(jnp.float32)[:, None, None]
    sign_z = (2 * (octant // 4) - 1).astype(jnp.float32)[:, None, None]
    angle = shift_phase * (sign_x * wave_x + sign_y * wave_y + sign_z * wave_z)
    angle = angle.reshape(8, TP * PP)
    return jnp.cos(angle), jnp.sin(angle)


def aggregate(child_fields):
    theta_up = interp_matrix(TP, TC, 0.5)
    phi_up = interp_matrix(PP, PC, 0.0)
    cosines, sines = phase_tables()
    fields = child_fields.reshape(-1, 2, TC, PC)
    wide_phi = jnp.einsum("bctp,jp->bctj", fields, phi_up, precision=lax.Precision.HIGHEST)
    wide = jnp.einsum("it,bctj->bcij", theta_up, wide_phi, precision=lax.Precision.HIGHEST)
    wide = wide.reshape(-1, 8, 2, TP * PP)
    real_part = wide[:, :, 0]
    imag_part = wide[:, :, 1]
    out_real = jnp.sum(cosines * real_part - sines * imag_part, axis=1)
    out_imag = jnp.sum(sines * real_part + cosines * imag_part, axis=1)
    return jnp.stack([out_real, out_imag], axis=1)


def disaggregate(parent_fields):
    theta_up = interp_matrix(TP, TC, 0.5)
    phi_up = interp_matrix(PP, PC, 0.0)
    cosines, sines = phase_tables()
    real_part = parent_fields[:, None, 0]
    imag_part = parent_fields[:, None, 1]
    turned_real = cosines * real_part + sines * imag_part
    turned_imag = cosines * imag_part - sines * real_part
    turned = jnp.stack([turned_real, turned_imag], axis=2).reshape(-1, 8, 2, TP, PP)
    narrow_theta = jnp.einsum("it,bocij->boctj", theta_up, turned, precision=lax.Precision.HIGHEST)
    narrow = jnp.einsum("boctj,jp->boctp", narrow_theta, phi_up, precision=lax.Precision.HIGHEST)
    narrow = narrow * ((TC * PC) / (TP * PP))
    return narrow.reshape(-1, 2, TC * PC)


def translate(source_pool, slot_index, table_index, counts, trans_table, block_size):
    group_size, far_length = slot_index.shape

    def one_block(operands):
        source_rows, table_rows, live_counts = operands
        fields = source_pool[source_rows]
        tables = trans_table[table_rows]
        live_mask = (jnp.arange(far_length, dtype=jnp.int32)[None, :] < live_counts[:, None]).astype(jnp.float32)[:, :, None]
        real_sum = jnp.sum(live_mask * (fields[:, :, 0] * tables[:, :, 0] - fields[:, :, 1] * tables[:, :, 1]), axis=1)
        imag_sum = jnp.sum(live_mask * (fields[:, :, 0] * tables[:, :, 1] + fields[:, :, 1] * tables[:, :, 0]), axis=1)
        return jnp.stack([real_sum, imag_sum], axis=1)

    result = lax.map(one_block, (slot_index.reshape(-1, block_size, far_length), table_index.reshape(-1, block_size, far_length), counts.reshape(-1, block_size)))
    return result.reshape(group_size, 2, -1)


def reference(child_outgoing, trans_table, send_rows, far_slot, far_trans, far_count):
    parent_outgoing = aggregate(child_outgoing)
    target_group = (jnp.arange(PARENTS, dtype=jnp.int32) // PG).astype(jnp.int32)
    source_group = (far_slot // CAP).astype(jnp.int32)
    source_pos = (far_slot % CAP).astype(jnp.int32)
    source_local = send_rows[source_group, target_group[:, None], source_pos]
    source_parent = (source_group * PG + source_local).astype(jnp.int32)
    block_size = math.gcd(PARENTS, 8)
    parent_incoming = translate(parent_outgoing, source_parent, far_trans, far_count, trans_table, block_size)
    return disaggregate(parent_incoming)
```

```python
import functools
import math

import jax
import jax.numpy as jnp
import numpy as np
from jax import lax
from jax.experimental import pallas as pl
from jax.experimental.pallas import tpu as pltpu
from jax.sharding import PartitionSpec as P

TC = 32
PC = 64
TP = 64
PP = 128
NTRANS = 316
NFAR = 189
CAP = 32
GROUPS = 16
SHIFT_PHASE = 2.7

NX = 8
NY = 8
NZ = 8
BF = jnp.bfloat16
MESH = pl.DeviceIdType.MESH


def interp_matrix(count_out, count_in, offset):
    target = (np.arange(count_out) + offset) / count_out
    source = (np.arange(count_in) + offset) / count_in
    spread = target[:, None] - source[None, :]
    orders = np.arange(1, count_in // 2)
    series = np.sum(np.cos(2.0 * math.pi * orders[None, None, :] * spread[:, :, None]), axis=2)
    return (1.0 + 2.0 * series + np.cos(math.pi * count_in * spread)) / count_in


def phase_tables():
    polar = math.pi * (np.arange(TP) + 0.5) / TP
    azimuth = 2.0 * math.pi * np.arange(PP) / PP
    wave_x = np.sin(polar)[:, None] * np.cos(azimuth)[None, :]
    wave_y = np.sin(polar)[:, None] * np.sin(azimuth)[None, :]
    wave_z = np.cos(polar)[:, None] * np.ones((1, PP))
    octant = np.arange(8)
    sign_x = (2 * (octant % 2) - 1)[:, None, None]
    sign_y = (2 * (octant // 2 % 2) - 1)[:, None, None]
    sign_z = (2 * (octant // 4) - 1)[:, None, None]
    angle = SHIFT_PHASE * (sign_x * wave_x + sign_y * wave_y + sign_z * wave_z)
    return np.cos(angle), np.sin(angle)


def halves(matrix):
    high = np.asarray(matrix, np.float32).astype(BF)
    low = (np.asarray(matrix, np.float32) - high.astype(np.float32)).astype(BF)
    return high, low


def constants():
    theta = interp_matrix(TP, TC, 0.5)
    phi = interp_matrix(PP, PC, 0.0)
    cosines, sines = phase_tables()
    pair = np.zeros((128, 256))
    pair[:64, :128] = phi.T
    pair[64:, 128:] = phi.T
    high, low = halves(pair)
    phi_out = np.concatenate([high, high, low], axis=0)
    theta_ba = np.concatenate([theta[:, 0::2], theta[:, 1::2]], axis=1)
    high, low = halves(theta_ba)
    theta_out = np.concatenate([high, high, low], axis=1)
    order = np.arange(64).reshape(8, 8).T.reshape(-1)
    high, low = halves(theta_ba.T[:, order])
    theta_in = np.concatenate([high, high, low], axis=1)
    back = np.zeros((256, 128))
    back[:128, :64] = phi
    back[128:, 64:] = phi
    high, low = halves(back * (TC * PC / (TP * PP)))
    phi_in = np.concatenate([high, high, low], axis=0)
    f32 = np.float32
    return dict(
        phi_out=phi_out, theta_out=theta_out, cos_out=cosines.astype(f32), sin_out=sines.astype(f32),
        theta_in=theta_in, phi_in=phi_in, cos_in=cosines[:, order].astype(f32), sin_in=sines[:, order].astype(f32),
    )


def split(value):
    high = value.astype(BF)
    low = (value - high.astype(jnp.float32)).astype(BF)
    return high, low


def position():
    b = lax.axis_index("boxes")
    d = lax.axis_index("dirs")
    return b, b // 2, b % 2, d // NZ, d % NZ


def signal(barrier, device):
    pl.semaphore_signal(barrier, inc=1, device_id=device, device_id_type=MESH)


def exchange(send0, recv1, send2, last, sems, b, y, z):
    ssem1, rsem1, ssem2, rsem2 = sems

    def along_y(k, peer_slot):
        target = (y + k) % NY
        return pltpu.make_async_remote_copy(
            src_ref=send0.at[pl.ds(pl.multiple_of(target * 16, 16), 16)],
            dst_ref=recv1.at[pl.ds(pl.multiple_of(peer_slot * 16, 16), 16)],
            send_sem=ssem1.at[k - 1], recv_sem=rsem1.at[k - 1],
            device_id=(b, target * NZ + z), device_id_type=MESH)

    for k in range(1, NY):
        along_y(k, y).start()
    mine = pl.ds(pl.multiple_of(y * 16, 16), 16)
    recv1[mine, :] = send0[mine, :]
    for k in range(1, NY):
        along_y(k, (y + NY - k) % NY).wait_recv()
    for target in range(NZ):
        for r in range(2):
            send2[target, r] = recv1[pl.ds(r * 8 + target, 8, stride=16), :]

    def along_z(k, peer_slot):
        target = (z + k) % NZ
        return pltpu.make_async_remote_copy(
            src_ref=send2.at[target], dst_ref=last.at[peer_slot],
            send_sem=ssem2.at[k - 1], recv_sem=rsem2.at[k - 1],
            device_id=(b, y * NZ + target), device_id_type=MESH)

    for k in range(1, NZ):
        along_z(k, z).start()
    last[z] = send2[z]
    for k in range(1, NZ):
        along_z(k, (z + NZ - k) % NZ).wait_recv()

    def drain():
        for k in range(1, NY):
            along_y(k, y).wait_send()
        for k in range(1, NZ):
            along_z(k, z).wait_send()
    return drain


def out_kernel(x_ref, phi_ref, theta_ref, cos_ref, sin_ref, pool_ref,
               wide_phi, send0, recv1, send2, ssem1, rsem1, ssem2, rsem2, ssem3, rsem3, ssem4, rsem4):
    b, x, core, y, z = position()
    barrier = pltpu.get_barrier_semaphore()
    for k in range(1, NY):
        signal(barrier, (b, (y + k) % NY * NZ + z))
    for k in range(1, NZ):
        signal(barrier, (b, y * NZ + (z + k) % NZ))
    d = y * NZ + z
    right = (x + 1) % NX * 2 + core
    left = (x + NX - 1) % NX * 2 + core
    other = x * 2 + 1 - core
    for device in (right, left, other):
        signal(barrier, (device, d))

    high, low = split(x_ref[...])
    both = jnp.dot(jnp.concatenate([high, low, high], axis=1), phi_ref[...],
                   preferred_element_type=jnp.float32)
    wide_phi[:256, :] = both[:, :128]
    wide_phi[256:, :] = both[:, 128:]
    real = jnp.zeros((TP, PP), jnp.float32)
    imag = jnp.zeros((TP, PP), jnp.float32)
    for o in range(8):
        parts = []
        for r in range(2):
            parts.append(jnp.concatenate(
                [wide_phi[pl.ds(half * 256 + o * 32 + r, 16, stride=2), :] for half in range(2)], axis=0))
        high, low = split(jnp.concatenate(parts, axis=1))
        wide = jnp.dot(theta_ref[...], jnp.concatenate([high, low, high], axis=0),
                       preferred_element_type=jnp.float32)
        cosine, sine = cos_ref[o], sin_ref[o]
        real += cosine * wide[:, :128] - sine * wide[:, 128:]
        imag += sine * wide[:, :128] + cosine * wide[:, 128:]
    for i in range(NY):
        send0[i * 16:i * 16 + 8, :] = real[i * 8:i * 8 + 8]
        send0[i * 16 + 8:i * 16 + 16, :] = imag[i * 8:i * 8 + 8]

    pl.semaphore_wait(barrier, NY + NZ - 2 + 3)
    drain = exchange(send0, recv1, send2, pool_ref.at[b], (ssem1, rsem1, ssem2, rsem2), b, y, z)

    def part(h):
        return pl.ds(h * 4, 4)

    steps = [(s, h) for s in range(3) for h in range(2)]
    slots = steps + [(3, 0)]

    def ring(way, n, sent):
        s, h = slots[n]
        h = way if s == 3 else h
        back = s if sent else s + 1
        origin = (x + NX - back) % NX if way == 0 else (x + back) % NX
        block = pool_ref.at[origin * 2 + core, part(h)]
        return pltpu.make_async_remote_copy(
            src_ref=block, dst_ref=block, send_sem=ssem3.at[way, n], recv_sem=rsem3.at[way, n],
            device_id=((right, left)[way], d), device_id_type=MESH), origin, h

    def across(n, origin, h, mine):
        block = pool_ref.at[origin * 2 + (core if mine else 1 - core), part(h)]
        return pltpu.make_async_remote_copy(
            src_ref=block, dst_ref=block, send_sem=ssem4.at[n], recv_sem=rsem4.at[n],
            device_id=(other, d), device_id_type=MESH)

    crossed = []
    for n in range(2):
        ring(0, n, True)[0].start()
        ring(1, n, True)[0].start()
    for h in range(2):
        across(len(crossed), x, h, True).start()
        crossed.append((x, h))
    for n in range(7):
        for way in range(2):
            copy, origin, h = ring(way, n, False)
            copy.wait_recv()
            s, half = slots[n]
            if s < 2 or (s == 2 and half == way):
                after = slots.index((s + 1, half)) if s < 2 else 6
                ring(way, after, True)[0].start()
            across(len(crossed), origin, h, True).start()
            crossed.append((origin, h))
    for n, (origin, h) in enumerate(crossed):
        across(n, origin, h, False).wait_recv()
    drain()
    for n in range(7):
        for way in range(2):
            ring(way, n, True)[0].wait_send()
    for n, (origin, h) in enumerate(crossed):
        across(n, origin, h, True).wait_send()


def translate_kernel(count_hbm, slot_hbm, trans_hbm, rows_ref, pool_ref, table_ref, out_ref,
                     source4, slots4, table4, acc, count_ref, slot_ref, trans_ref, sems):
    copies = [pltpu.make_async_copy(src, dst, sems.at[i]) for i, (src, dst) in enumerate(
        [(count_hbm, count_ref), (slot_hbm, slot_ref), (trans_hbm, trans_ref)])]
    for copy in copies:
        copy.start()
    for v in range(0, NTRANS, 8):
        n = min(8, NTRANS - v)
        for r in range(2):
            rows = table_ref[pl.ds(v * 2 + r, n, stride=2), :]
            table4[pl.ds(v * 4 + 2 * r, n, stride=4), :] = rows
            table4[pl.ds(v * 4 + 2 * r + 1, n, stride=4), :] = rows
    for i in range(GROUPS * 8):
        for r in range(2):
            rows = pool_ref[i * 16 + r * 8:i * 16 + r * 8 + 8, :]
            source4[pl.ds(i * 32 + r, 8, stride=4), :] = rows
            source4[pl.ds(i * 32 + r + 2, 8, stride=4), :] = rows

    def pick(i, carry):
        for j in range(8):
            s = i * 8 + j
            m = rows_ref[s]
            row = s // CAP * 64 + m % 8 * 8 + m // 8
            slots4[s] = source4[pl.ds(pl.multiple_of(row * 4, 4), 4), :]
        return carry

    lax.fori_loop(0, GROUPS * CAP // 8, pick, 0)
    for copy in copies:
        copy.wait()

    def one_target(t, carry):
        count = count_ref[t]

        def turn(width, base, limit, sums):
            sums = list(sums)
            for j in range(width):
                e = base + j
                value = slots4[slot_ref[t, e]] * table4[pl.ds(pl.multiple_of(trans_ref[t, e] * 4, 4), 4), :]
                if limit is not None:
                    value = jnp.where(e < limit, value, 0.0)
                sums[j % 4] = sums[j % 4] + value
            return tuple(sums)

        zero = jnp.zeros((4, 128), jnp.float32)
        wide = count // 32
        sums = lax.fori_loop(0, wide, lambda i, c: turn(32, i * 32, None, c), (zero,) * 4)
        base = wide * 32
        full = (count - base) // 8
        sums = lax.fori_loop(0, full, lambda i, c: turn(8, base + i * 8, None, c), sums)
        base = base + full * 8

        def single(e, c):
            return (c[0] + slots4[slot_ref[t, e]] * table4[pl.ds(pl.multiple_of(trans_ref[t, e] * 4, 4), 4), :],) + c[1:]
        sums = lax.fori_loop(base, count, single, sums)
        acc[t] = (sums[0] + sums[1]) + (sums[2] + sums[3])
        return carry

    lax.fori_loop(0, 64, one_target, 0)
    for i in range(8):
        q = [acc[i * 8:i * 8 + 8, k, :] for k in range(4)]
        out_ref[i * 16:i * 16 + 8, :] = q[0] - q[3]
        out_ref[i * 16 + 8:i * 16 + 16, :] = q[1] + q[2]


def in_kernel(field_ref, phi_ref, theta_ref, cos_ref, sin_ref, out_ref,
              recv1, send2, last, ssem1, rsem1, ssem2, rsem2):
    b, x, core, y, z = position()
    barrier = pltpu.get_barrier_semaphore()
    for k in range(1, NY):
        signal(barrier, (b, (y + k) % NY * NZ + z))
    for k in range(1, NZ):
        signal(barrier, (b, y * NZ + (z + k) % NZ))
    pl.semaphore_wait(barrier, NY + NZ - 2)
    drain = exchange(field_ref, recv1, send2, last, (ssem1, rsem1, ssem2, rsem2), b, y, z)
    real = last[:, 0].reshape(TP, PP)
    imag = last[:, 1].reshape(TP, PP)
    narrow = []
    for o in range(8):
        cosine, sine = cos_ref[o], sin_ref[o]
        high, low = split(jnp.concatenate([cosine * real + sine * imag, cosine * imag - sine * real], axis=1))
        rows = jnp.dot(theta_ref[...], jnp.concatenate([high, low, high], axis=0),
                       preferred_element_type=jnp.float32)
        for r in range(2):
            cols = rows[:, r * 128:(r + 1) * 128]
            narrow.append(jnp.concatenate([cols[:16], cols[16:]], axis=1))
    high, low = split(jnp.concatenate(narrow, axis=0))
    result = jnp.dot(jnp.concatenate([high, low, high], axis=1), phi_ref[...],
                     preferred_element_type=jnp.float32)
    for o in range(8):
        for r in range(2):
            n = o * 2 + r
            out_ref[pl.ds(o * 32 + r, 16, stride=2), :] = result[n * 16:(n + 1) * 16]
    drain()


def whole():
    return pl.BlockSpec(memory_space=pltpu.VMEM)


def dma(*shape):
    return pltpu.SemaphoreType.DMA(shape)


def outgoing_pool(fields, const):
    f32 = jnp.float32
    return pl.pallas_call(
        out_kernel,
        out_shape=jax.ShapeDtypeStruct((GROUPS, NZ, 2, NY, 128), f32),
        in_specs=[whole()] * 5, out_specs=whole(),
        scratch_shapes=[pltpu.VMEM((512, 128), f32), pltpu.VMEM((128, 128), f32), pltpu.VMEM((128, 128), f32),
                        pltpu.VMEM((NZ, 2, NY, 128), f32),
                        dma(7), dma(7), dma(7), dma(7), dma(2, 7), dma(2, 7), dma(16), dma(16)],
        compiler_params=pltpu.CompilerParams(collective_id=0, has_side_effects=True, vmem_limit_bytes=32 << 20),
        name="outgoing",
    )(fields, const["phi_out"], const["theta_out"], const["cos_out"], const["sin_out"])


def translate(counts, slots, trans, rows, pool, table):
    f32 = jnp.float32
    smem = pl.BlockSpec(memory_space=pltpu.SMEM)
    raw = pl.BlockSpec(memory_space=pl.ANY)
    return pl.pallas_call(
        translate_kernel,
        out_shape=jax.ShapeDtypeStruct((128, 128), f32),
        in_specs=[raw, raw, raw, smem, whole(), whole()], out_specs=whole(),
        scratch_shapes=[pltpu.VMEM((GROUPS * 64 * 4, 128), f32), pltpu.VMEM((GROUPS * CAP, 4, 128), f32),
                        pltpu.VMEM((NTRANS * 4, 128), f32), pltpu.VMEM((64, 4, 128), f32),
                        pltpu.SMEM((64,), jnp.int32), pltpu.SMEM((64, NFAR), jnp.int32),
                        pltpu.SMEM((64, NFAR), jnp.int32), dma(3)],
        compiler_params=pltpu.CompilerParams(vmem_limit_bytes=32 << 20),
        name="translate",
    )(counts, slots, trans, rows, pool, table)


def incoming_fields(field, const):
    f32 = jnp.float32
    return pl.pallas_call(
        in_kernel,
        out_shape=jax.ShapeDtypeStruct((256, 128), f32),
        in_specs=[whole()] * 5, out_specs=whole(),
        scratch_shapes=[pltpu.VMEM((128, 128), f32), pltpu.VMEM((NZ, 2, NY, 128), f32), pltpu.VMEM((NZ, 2, NY, 128), f32),
                        dma(7), dma(7), dma(7), dma(7)],
        compiler_params=pltpu.CompilerParams(collective_id=1, has_side_effects=True, vmem_limit_bytes=32 << 20),
        name="incoming",
    )(field, const["phi_in"], const["theta_in"], const["cos_in"], const["sin_in"])


def on_device(const, child_outgoing, trans_table, send_rows, far_slot, far_trans, far_count):
    fields = child_outgoing.reshape(8, 2, 16, 128).transpose(0, 2, 1, 3).reshape(256, 128)
    pool = outgoing_pool(fields, const)
    rows = lax.dynamic_index_in_dim(send_rows, lax.axis_index("boxes"), 1, keepdims=False).reshape(GROUPS * CAP)
    field = translate(far_count, far_slot, far_trans, rows, pool.reshape(GROUPS * 128, 128),
                      trans_table.reshape(NTRANS * 2, 128))
    out = incoming_fields(field, const)
    return out.reshape(8, 16, 2, 128).transpose(0, 2, 1, 3).reshape(8, 2, 2048)


def solution(mesh):
    placed = (
        P(("boxes", "dirs"), None, None),
        P(None, None, "dirs"),
        P(),
        P("boxes", None),
        P("boxes", None),
        P("boxes"),
    )
    const = {name: np.asarray(value) for name, value in constants().items()}
    return jax.shard_map(
        functools.partial(on_device, const),
        mesh=mesh,
        in_specs=placed,
        out_specs=P(("boxes", "dirs"), None, None),
        check_vma=False,
    )
```

```python
import functools
import math

import jax
import jax.numpy as jnp
import numpy as np
from jax import lax
from jax.experimental import pallas as pl
from jax.experimental.pallas import tpu as pltpu
from jax.sharding import PartitionSpec as P

TC = 32
PC = 64
TP = 64
PP = 128
NTRANS = 316
NFAR = 189
CAP = 32
GROUPS = 16
SHIFT_PHASE = 2.7

NX = 8
NY = 8
NZ = 8
BF = jnp.bfloat16
MESH = pl.DeviceIdType.MESH


def interp_matrix(count_out, count_in, offset):
    target = (np.arange(count_out) + offset) / count_out
    source = (np.arange(count_in) + offset) / count_in
    spread = target[:, None] - source[None, :]
    orders = np.arange(1, count_in // 2)
    series = np.sum(np.cos(2.0 * math.pi * orders[None, None, :] * spread[:, :, None]), axis=2)
    return (1.0 + 2.0 * series + np.cos(math.pi * count_in * spread)) / count_in


def phase_tables():
    polar = math.pi * (np.arange(TP) + 0.5) / TP
    azimuth = 2.0 * math.pi * np.arange(PP) / PP
    wave_x = np.sin(polar)[:, None] * np.cos(azimuth)[None, :]
    wave_y = np.sin(polar)[:, None] * np.sin(azimuth)[None, :]
    wave_z = np.cos(polar)[:, None] * np.ones((1, PP))
    octant = np.arange(8)
    sign_x = (2 * (octant % 2) - 1)[:, None, None]
    sign_y = (2 * (octant // 2 % 2) - 1)[:, None, None]
    sign_z = (2 * (octant // 4) - 1)[:, None, None]
    angle = SHIFT_PHASE * (sign_x * wave_x + sign_y * wave_y + sign_z * wave_z)
    return np.cos(angle), np.sin(angle)


def halves(matrix):
    high = np.asarray(matrix, np.float32).astype(BF)
    low = (np.asarray(matrix, np.float32) - high.astype(np.float32)).astype(BF)
    return high, low


def constants():
    theta = interp_matrix(TP, TC, 0.5)
    phi = interp_matrix(PP, PC, 0.0)
    cosines, sines = phase_tables()
    pair = np.zeros((128, 256))
    pair[:64, :128] = phi.T
    pair[64:, 128:] = phi.T
    high, low = halves(pair)
    phi_out = np.concatenate([high, high, low], axis=0)
    theta_ba = np.concatenate([theta[:, 0::2], theta[:, 1::2]], axis=1)
    high, low = halves(theta_ba)
    theta_out = np.concatenate([high, high, low], axis=1)
    order = np.arange(64).reshape(8, 8).T.reshape(-1)
    high, low = halves(theta_ba.T[:, order])
    theta_in = np.concatenate([high, high, low], axis=1)
    back = np.zeros((256, 128))
    back[:128, :64] = phi
    back[128:, 64:] = phi
    high, low = halves(back * (TC * PC / (TP * PP)))
    phi_in = np.concatenate([high, high, low], axis=0)
    tables = np.concatenate([cosines[:4].reshape(256, 128), sines[:4].reshape(256, 128)]).astype(np.float32)
    return phi_out, theta_out, tables, theta_in, phi_in


def split(value):
    high = value.astype(BF)
    low = (value - high.astype(jnp.float32)).astype(BF)
    return high, low


def position():
    b = lax.axis_index("boxes")
    d = lax.axis_index("dirs")
    return b, b // 2, b % 2, d // NZ, d % NZ


def signal(barrier, device):
    pl.semaphore_signal(barrier, inc=1, device_id=device, device_id_type=MESH)


def one_hot(columns, first, tiles):
    lanes = lax.broadcasted_iota(jnp.int32, (16, 128), 1)
    numbers = [(lanes + (128 * k - first)).astype(jnp.float32).astype(BF) for k in range(tiles)]
    one, zero = jnp.ones((16, 128), BF), jnp.zeros((16, 128), BF)
    rows = []
    for e in range(0, 64, 2):
        column = jnp.concatenate([jnp.broadcast_to(columns[:, e + j:e + j + 1], (8, 128)) for j in range(2)], axis=0)
        column = column.astype(BF)
        rows.append([jnp.where(column == number, one, zero) for number in numbers])
    pieces = [jnp.concatenate([row[k] for row in rows], axis=0) for k in range(tiles)]
    return jnp.concatenate(pieces + pieces, axis=1)


def kernel(x_hbm, table_hbm, send_hbm, slot_hbm, trans_hbm, count_hbm, phi_out_hbm, theta_out_hbm, phases_hbm,
           theta_in_hbm, phi_in_hbm, out_ref,
           x_ref, table_ref, send_ref, slot_ref, trans_ref, count_ref, phi_out, theta_out, phases, theta_in, phi_in,
           wide_phi, send0, recv1, send2, pool, slot_at, trans_at, chosen, pick, sources, tables, gathered,
           back0, back1, back2, last, load_sem,
           ssem1, rsem1, ssem2, rsem2, ssem3, rsem3, ssem4, rsem4, ssem5, rsem5, ssem6, rsem6):
    f32 = jnp.float32
    b, x, core, y, z = position()
    d = y * NZ + z
    right = (x + 1) % NX * 2 + core
    left = (x + NX - 1) % NX * 2 + core
    other = x * 2 + 1 - core
    barrier = pltpu.get_barrier_semaphore()
    for k in range(1, NY):
        signal(barrier, (b, (y + k) % NY * NZ + z))
    for k in range(1, NZ):
        signal(barrier, (b, y * NZ + (z + k) % NZ))
    for device in (right, left, other):
        signal(barrier, (device, d))
    pairs = [(x_hbm, x_ref), (phi_out_hbm, phi_out), (theta_out_hbm, theta_out), (phases_hbm, phases),
             (table_hbm, table_ref.at[pl.ds(0, 2 * NTRANS)]), (trans_hbm, trans_ref), (count_hbm, count_ref),
             (slot_hbm, slot_ref), (send_hbm, send_ref), (theta_in_hbm, theta_in), (phi_in_hbm, phi_in)]
    loads = [pltpu.make_async_copy(src, dst, load_sem.at[i]) for i, (src, dst) in enumerate(pairs)]
    for load in loads:
        load.start()

    loads[0].wait()
    loads[1].wait()
    high, low = split(x_ref[...])
    both = jnp.dot(jnp.concatenate([high, low, high], axis=1), phi_out[...], preferred_element_type=f32)
    wide_phi[:256, :] = both[:, :128]
    wide_phi[256:, :] = both[:, 128:]
    loads[2].wait()
    loads[3].wait()
    real = jnp.zeros((TP, PP), f32)
    imag = jnp.zeros((TP, PP), f32)

    def child(o, r):
        return jnp.concatenate([wide_phi[pl.ds(half * 256 + o * 32 + r, 16, stride=2), :] for half in range(2)], axis=0)

    for o in range(4):
        near = [child(o, r) for r in range(2)]
        far = [child(7 - o, r) for r in range(2)]
        high, low = split(jnp.concatenate(
            [near[0] + far[0], near[1] + far[1], near[0] - far[0], near[1] - far[1]], axis=1))
        wide = jnp.dot(theta_out[...], jnp.concatenate([high, low, high], axis=0), preferred_element_type=f32)
        cosine, sine = phases[o * 64:o * 64 + 64, :], phases[256 + o * 64:256 + o * 64 + 64, :]
        real += cosine * wide[:, :128] - sine * wide[:, 384:]
        imag += sine * wide[:, 256:384] + cosine * wide[:, 128:256]
    for i in range(NY):
        send0[i * 16:i * 16 + 8, :] = real[i * 8:i * 8 + 8]
        send0[i * 16 + 8:i * 16 + 16, :] = imag[i * 8:i * 8 + 8]

    pl.semaphore_wait(barrier, NY + NZ - 2 + 3)

    def along_y(source, landing, ssem, rsem, k, peer_slot):
        target = (y + k) % NY
        return pltpu.make_async_remote_copy(
            src_ref=source.at[pl.ds(pl.multiple_of(target * 16, 16), 16)],
            dst_ref=landing.at[pl.ds(pl.multiple_of(peer_slot * 16, 16), 16)],
            send_sem=ssem.at[k], recv_sem=rsem.at[k],
            device_id=(b, target * NZ + z), device_id_type=MESH)

    def along_z(source, landing, ssem, rsem, k, peer_slot):
        target = (z + k) % NZ
        return pltpu.make_async_remote_copy(
            src_ref=source.at[target], dst_ref=landing.at[peer_slot],
            send_sem=ssem.at[k], recv_sem=rsem.at[k],
            device_id=(b, y * NZ + target), device_id_type=MESH)

    far_first = (4, 3, 5, 2, 6, 1, 7)
    for k in far_first:
        along_y(send0, recv1, ssem1, rsem1, k, y).start()
    mine = pl.ds(pl.multiple_of(y * 16, 16), 16)
    recv1[mine, :] = send0[mine, :]

    table_ref[2 * NTRANS:, :] = jnp.zeros((768 - 2 * NTRANS, 128), f32)
    for i in range(4, 7):
        loads[i].wait()
    for r in range(2):
        high, low = split(table_ref[pl.ds(r, 384, stride=2), :])
        tables[:384, r * 128:(r + 1) * 128] = high
        tables[384:, r * 128:(r + 1) * 128] = low
    diagonal = lax.broadcasted_iota(jnp.int32, (64, 64), 0) == lax.broadcasted_iota(jnp.int32, (64, 64), 1)
    count = jnp.broadcast_to(count_ref[...].astype(f32), (64, 64))
    count = jnp.sum(jnp.where(diagonal, count, 0.0), axis=1, keepdims=True)
    entry = lax.broadcasted_iota(jnp.int32, (64, NFAR), 1).astype(f32)
    trans_at[...] = jnp.full((64, 256), -256.0, f32)
    trans_at[:, :NFAR] = jnp.where(entry < count, (trans_ref[...] - 158).astype(f32), -256.0)

    def gather_tables(i, carry):
        columns = trans_at[pl.ds(pl.multiple_of(i * 8, 8), 8), :]
        for chunk in range(3):
            rows = pl.ds(pl.multiple_of((i * 3 + chunk) * 512, 512), 512)
            gathered[rows, :] = jnp.dot(one_hot(columns[:, chunk * 64:chunk * 64 + 64], 158, 3), tables[...],
                                        preferred_element_type=f32)
        return carry

    lax.fori_loop(0, 3, gather_tables, 0)
    for k in range(1, NY):
        along_y(send0, recv1, ssem1, rsem1, k, (y + NY - k) % NY).wait_recv()
    for target in range(NZ):
        for r in range(2):
            send2[target, r] = recv1[pl.ds(r * 8 + target, 8, stride=16), :]
    for k in far_first:
        along_z(send2, pool.at[b], ssem2, rsem2, k, z).start()
    pool[b, z] = send2[z]

    loads[7].wait()
    loads[8].wait()
    slot_at[...] = jnp.zeros((64, 256), f32)
    slot_at[:, :NFAR] = (slot_ref[...] - 256).astype(f32)
    chosen[...] = jnp.zeros((16, 128), f32)
    for g in range(GROUPS):
        chosen[g:g + 1, :CAP] = send_ref[g, pl.ds(b, 1), :].astype(f32)
    across_rows = chosen[...].T
    place = lax.broadcasted_iota(jnp.int32, (CAP, 64), 1)
    place = (place % 8 * 8 + place // 8).astype(f32)
    for g in range(GROUPS):
        pick[g * CAP:(g + 1) * CAP, :64] = jnp.where(
            jnp.broadcast_to(across_rows[:CAP, g:g + 1], (CAP, 64)) == place, 1.0, 0.0).astype(BF)
    lax.fori_loop(3, 6, gather_tables, 0)
    for k in range(1, NZ):
        along_z(send2, pool.at[b], ssem2, rsem2, k, (z + NZ - k) % NZ).wait_recv()

    def compact(g):
        block = pool[g]
        parts = [split(block[:, r].reshape(64, 128)) for r in range(2)]
        rows = pl.ds(pl.multiple_of(g * CAP, CAP), CAP)
        sent = jnp.dot(pick[rows, :64], jnp.concatenate([parts[0][0], parts[1][0], parts[0][1], parts[1][1]], axis=1),
                       preferred_element_type=f32).astype(BF)
        sources[rows, :] = sent[:, :256]
        sources[pl.ds(pl.multiple_of(512 + g * CAP, CAP), CAP), :] = sent[:, 256:]

    slots = [(s, h) for s in range(3) for h in range(2)] + [(3, 0)]

    def from_origin(way, back):
        return (x + NX - back) % NX if way == 0 else (x + back) % NX

    def ring(way, n, sent):
        s, h = slots[n]
        h = way if s == 3 else h
        block = pool.at[from_origin(way, s if sent else s + 1) * 2 + core, pl.ds(h * 4, 4)]
        return pltpu.make_async_remote_copy(
            src_ref=block, dst_ref=block, send_sem=ssem3.at[way, n], recv_sem=rsem3.at[way, n],
            device_id=((right, left)[way], d), device_id_type=MESH)

    def across(n, mine):
        if n == 0:
            back, way, part = 0, 0, pl.ds(0, 8)
        else:
            back, way = (n + 1) // 2, (n + 1) % 2
            part = pl.ds(0, 8) if back < 4 else pl.ds(way * 4, 4)
        block = pool.at[from_origin(way, back) * 2 + (core if mine else 1 - core), part]
        return pltpu.make_async_remote_copy(
            src_ref=block, dst_ref=block, send_sem=ssem4.at[n], recv_sem=rsem4.at[n],
            device_id=(other, d), device_id_type=MESH)

    for n in range(2):
        ring(0, n, True).start()
        ring(1, n, True).start()
    across(0, True).start()
    compact(b)
    lax.fori_loop(6, 8, gather_tables, 0)
    for s in range(4):
        for n, (step, h) in enumerate(slots):
            if step != s:
                continue
            for way in range(2):
                ring(way, n, False).wait_recv()
                if s < 2 or (s == 2 and h == way):
                    ring(way, n + 2 if s < 2 else 6, True).start()
        for way in range(2):
            across(2 * s + 1 + way, True).start()
        for way in range(2 if s < 3 else 1):
            compact(from_origin(way, s + 1) * 2 + core)
        for n in ((0,), (1, 2), (3, 4), (5, 6))[s]:
            across(n, False).wait_recv()
            way, back = (0, 0) if n == 0 else ((n + 1) % 2, (n + 1) // 2)
            compact(from_origin(way, back) * 2 + 1 - core)
    across(7, False).wait_recv()
    across(8, False).wait_recv()
    compact(from_origin(0, 4) * 2 + 1 - core)

    def one_owner(i, carry):
        k = 4 + (i + 1) // 2 * (1 - 2 * (i % 2))
        target = (y + k) % NY
        columns = slot_at[pl.ds(pl.multiple_of(target * 8, 8), 8), :]
        real = jnp.zeros((8, 128), f32)
        imag = jnp.zeros((8, 128), f32)
        for chunk in range(3):
            field = jnp.dot(one_hot(columns[:, chunk * 64:chunk * 64 + 64], 256, 4), sources[...],
                            preferred_element_type=f32)
            weight = gathered[pl.ds(pl.multiple_of((target * 3 + chunk) * 512, 512), 512), :]
            fr, fi, wr, wi = field[:, :128], field[:, 128:], weight[:, :128], weight[:, 128:]
            real += jnp.sum((fr * wr - fi * wi).reshape(64, 8, 128), axis=0)
            imag += jnp.sum((fr * wi + fi * wr).reshape(64, 8, 128), axis=0)
        back0[pl.ds(pl.multiple_of(target * 16, 16), 8), :] = real
        back0[pl.ds(pl.multiple_of(target * 16 + 8, 8), 8), :] = imag

        @pl.when(i < 7)
        def _():
            along_y(back0, back1, ssem5, rsem5, k, y).start()
        return carry

    lax.fori_loop(0, NY, one_owner, 0)
    back1[mine, :] = back0[mine, :]
    for load in loads[9:]:
        load.wait()
    for k in range(1, NY):
        along_y(back0, back1, ssem5, rsem5, k, (y + NY - k) % NY).wait_recv()
    for target in range(NZ):
        for r in range(2):
            back2[target, r] = back1[pl.ds(r * 8 + target, 8, stride=16), :]
    for k in far_first:
        along_z(back2, last, ssem6, rsem6, k, z).start()
    last[z] = back2[z]
    for k in range(1, NY):
        along_y(send0, recv1, ssem1, rsem1, k, y).wait_send()
        along_z(send2, pool.at[b], ssem2, rsem2, k, z).wait_send()
        along_y(back0, back1, ssem5, rsem5, k, y).wait_send()
    for n in range(7):
        for way in range(2):
            ring(way, n, True).wait_send()
    for n in range(9):
        across(n, True).wait_send()
    for k in range(1, NZ):
        along_z(back2, last, ssem6, rsem6, k, (z + NZ - k) % NZ).wait_recv()

    real = last[:, 0].reshape(TP, PP)
    imag = last[:, 1].reshape(TP, PP)
    narrow = [None] * 16
    for o in range(4):
        cosine, sine = [jnp.concatenate([phases[pl.ds(half * 256 + o * 64 + i, 8, stride=8), :] for i in range(NZ)], axis=0)
                        for half in range(2)]
        high, low = split(jnp.concatenate([cosine * real, sine * imag, cosine * imag, sine * real], axis=1))
        rows = jnp.dot(theta_in[...], jnp.concatenate([high, low, high], axis=0), preferred_element_type=f32)
        cr, si, ci, sr = [rows[:, i * 128:(i + 1) * 128] for i in range(4)]
        for n, value in ((o, cr + si), (7 - o, cr - si)):
            narrow[n * 2] = jnp.concatenate([value[:16], value[16:]], axis=1)
        for n, value in ((o, ci - sr), (7 - o, ci + sr)):
            narrow[n * 2 + 1] = jnp.concatenate([value[:16], value[16:]], axis=1)
    high, low = split(jnp.concatenate(narrow, axis=0))
    result = jnp.dot(jnp.concatenate([high, low, high], axis=1), phi_in[...], preferred_element_type=f32)
    for o in range(8):
        for r in range(2):
            n = o * 2 + r
            out_ref[pl.ds(o * 32 + r, 16, stride=2), :] = result[n * 16:(n + 1) * 16]
    for k in range(1, NZ):
        along_z(back2, last, ssem6, rsem6, k, z).wait_send()


def whole():
    return pl.BlockSpec(memory_space=pltpu.VMEM)


def dma(*shape):
    return pltpu.SemaphoreType.DMA(shape)


def whole_step(fields, table, send_rows, slots, trans, counts, const):
    f32, i32 = jnp.float32, jnp.int32
    vmem = pltpu.VMEM
    tile = (NZ, 2, NY, 128)
    return pl.pallas_call(
        kernel,
        out_shape=jax.ShapeDtypeStruct((256, 128), f32),
        in_specs=[pl.BlockSpec(memory_space=pl.ANY)] * 11, out_specs=whole(),
        scratch_shapes=[
            vmem((256, 128), f32), vmem((768, 128), f32), vmem((GROUPS, GROUPS, CAP), i32), vmem((64, NFAR), i32),
            vmem((64, NFAR), i32), vmem((1, 64), i32), vmem((384, 256), BF), vmem((64, 96), BF), vmem((512, 128), f32),
            vmem((32, 192), BF), vmem((768, 128), BF),
            vmem((512, 128), f32), vmem((128, 128), f32), vmem((128, 128), f32), vmem(tile, f32),
            vmem((GROUPS,) + tile, f32), vmem((64, 256), f32), vmem((64, 256), f32), vmem((16, 128), f32),
            vmem((GROUPS * CAP, 128), BF), vmem((2 * GROUPS * CAP, 256), BF), vmem((768, 256), BF),
            vmem((24 * 512, 256), f32),
            vmem((128, 128), f32), vmem((128, 128), f32), vmem(tile, f32), vmem(tile, f32), dma(11),
            dma(8), dma(8), dma(8), dma(8), dma(2, 7), dma(2, 7), dma(9), dma(9), dma(8), dma(8), dma(8), dma(8)],
        compiler_params=pltpu.CompilerParams(collective_id=0, has_side_effects=True, vmem_limit_bytes=60 << 20),
        name="level_pair",
    )(fields, table, send_rows, slots, trans, counts, *const)


def on_device(const, child_outgoing, trans_table, send_rows, far_slot, far_trans, far_count):
    fields = child_outgoing.reshape(8, 2, 16, 128).transpose(0, 2, 1, 3).reshape(256, 128)
    out = whole_step(fields, trans_table.reshape(NTRANS * 2, 128), send_rows, far_slot, far_trans,
                     far_count.reshape(1, 64), const)
    return out.reshape(8, 16, 2, 128).transpose(0, 2, 1, 3).reshape(8, 2, 2048)


def solution(mesh):
    placed = (
        P(("boxes", "dirs"), None, None),
        P(None, None, "dirs"),
        P(),
        P("boxes", None),
        P("boxes", None),
        P("boxes"),
    )
    const = constants()
    return jax.shard_map(
        functools.partial(on_device, const),
        mesh=mesh,
        in_specs=placed,
        out_specs=P(("boxes", "dirs"), None, None),
        check_vma=False,
    )
```

```python
import functools
import math

import jax
import jax.numpy as jnp
import numpy as np
from jax import lax
from jax.experimental import pallas as pl
from jax.experimental.pallas import tpu as pltpu
from jax.sharding import PartitionSpec as P

TC = 32
PC = 64
TP = 64
PP = 128
NTRANS = 316
NFAR = 189
CAP = 32
GROUPS = 16
SHIFT_PHASE = 2.7

NX = 8
NY = 8
NZ = 8
BF = jnp.bfloat16
MESH = pl.DeviceIdType.MESH
NEAR = (0, 1, 7, 2, 6, 3, 5, 4)


def interp_matrix(count_out, count_in, offset):
    target = (np.arange(count_out) + offset) / count_out
    source = (np.arange(count_in) + offset) / count_in
    spread = target[:, None] - source[None, :]
    orders = np.arange(1, count_in // 2)
    series = np.sum(np.cos(2.0 * math.pi * orders[None, None, :] * spread[:, :, None]), axis=2)
    return (1.0 + 2.0 * series + np.cos(math.pi * count_in * spread)) / count_in


def phase_tables():
    polar = math.pi * (np.arange(TP) + 0.5) / TP
    azimuth = 2.0 * math.pi * np.arange(PP) / PP
    wave_x = np.sin(polar)[:, None] * np.cos(azimuth)[None, :]
    wave_y = np.sin(polar)[:, None] * np.sin(azimuth)[None, :]
    wave_z = np.cos(polar)[:, None] * np.ones((1, PP))
    octant = np.arange(8)
    sign_x = (2 * (octant % 2) - 1)[:, None, None]
    sign_y = (2 * (octant // 2 % 2) - 1)[:, None, None]
    sign_z = (2 * (octant // 4) - 1)[:, None, None]
    angle = SHIFT_PHASE * (sign_x * wave_x + sign_y * wave_y + sign_z * wave_z)
    return np.cos(angle), np.sin(angle)


def halves(matrix):
    high = np.asarray(matrix, np.float32).astype(BF)
    low = (np.asarray(matrix, np.float32) - high.astype(np.float32)).astype(BF)
    return high, low


def constants():
    theta = interp_matrix(TP, TC, 0.5)
    phi = interp_matrix(PP, PC, 0.0)
    cosines, sines = phase_tables()
    pair = np.zeros((128, 256))
    pair[:64, :128] = phi.T
    pair[64:, 128:] = phi.T
    high, low = halves(pair)
    phi_out = np.concatenate([high, high, low], axis=0)
    theta_ba = np.concatenate([theta[:, 0::2], theta[:, 1::2]], axis=1)
    high, low = halves(theta_ba)
    theta_out = np.concatenate([high, high, low], axis=1)
    order = np.arange(64).reshape(8, 8).T.reshape(-1)
    high, low = halves(theta_ba.T[:, order])
    theta_in = np.concatenate([high, high, low], axis=1)
    back = np.zeros((256, 128))
    back[:128, :64] = phi
    back[128:, 64:] = phi
    high, low = halves(back * (TC * PC / (TP * PP)))
    phi_in = np.concatenate([high, high, low], axis=0)
    tables = np.concatenate([cosines[:4].reshape(256, 128), sines[:4].reshape(256, 128)]).astype(np.float32)
    return phi_out, theta_out, tables, theta_in, phi_in


def split(value):
    high = value.astype(BF)
    low = (value - high.astype(jnp.float32)).astype(BF)
    return high, low


def position():
    b = lax.axis_index("boxes")
    d = lax.axis_index("dirs")
    return b, b // 2, b % 2, d // NZ, d % NZ


def signal(barrier, device):
    pl.semaphore_signal(barrier, inc=1, device_id=device, device_id_type=MESH)


def one_hot(columns, first, tiles):
    lanes = lax.broadcasted_iota(jnp.int32, (16, 128), 1)
    numbers = [(lanes + (128 * k - first)).astype(jnp.float32).astype(BF) for k in range(tiles)]
    one, zero = jnp.ones((16, 128), BF), jnp.zeros((16, 128), BF)
    rows = []
    for e in range(0, 64, 2):
        column = jnp.concatenate([jnp.broadcast_to(columns[:, e + j:e + j + 1], (8, 128)) for j in range(2)], axis=0)
        column = column.astype(BF)
        rows.append([jnp.where(column == number, one, zero) for number in numbers])
    pieces = [jnp.concatenate([row[k] for row in rows], axis=0) for k in range(tiles)]
    return jnp.concatenate(pieces + pieces, axis=1)


def by_chunk(ref, lists, fill):
    for chunk in range(3):
        width = min(64, NFAR - chunk * 64)
        ref[chunk * 64:chunk * 64 + 64, :] = jnp.full((64, 128), fill, jnp.float32)
        ref[chunk * 64:chunk * 64 + 64, :width] = lists[:, chunk * 64:chunk * 64 + width]


def kernel(x_hbm, table_hbm, send_hbm, slot_hbm, trans_hbm, count_hbm, phi_out_hbm, theta_out_hbm, phases_hbm,
           theta_in_hbm, phi_in_hbm, out_ref,
           x_ref, table_ref, send_ref, slot_ref, trans_ref, count_ref, phi_out, theta_out, phases, theta_in, phi_in,
           wide_phi, send0, recv1, send2, pool, slot_at, trans_at, chosen, pick, sources, tables, gathered,
           halfway, back0, back1, back2, last, load_sem,
           ssem1, rsem1, ssem2, rsem2, ssem3, rsem3, ssem4, rsem4, ssem5, rsem5, ssem6, rsem6):
    f32 = jnp.float32
    b, x, core, y, z = position()
    d = y * NZ + z
    right = (x + 1) % NX * 2 + core
    left = (x + NX - 1) % NX * 2 + core
    other = x * 2 + 1 - core
    barrier = pltpu.get_barrier_semaphore()
    far_first = (4, 3, 5, 2, 6, 1, 7)
    for k in far_first:
        signal(barrier, (b, (y + k) % NY * NZ + z))
        signal(barrier, (b, y * NZ + (z + k) % NZ))
    for device in (right, left, other):
        signal(barrier, (device, d))
    pairs = [(x_hbm, x_ref), (phi_out_hbm, phi_out), (theta_out_hbm, theta_out), (phases_hbm, phases),
             (table_hbm, table_ref.at[pl.ds(0, 2 * NTRANS)]), (trans_hbm, trans_ref), (count_hbm, count_ref),
             (slot_hbm, slot_ref), (send_hbm, send_ref), (theta_in_hbm, theta_in), (phi_in_hbm, phi_in)]
    loads = [pltpu.make_async_copy(src, dst, load_sem.at[i]) for i, (src, dst) in enumerate(pairs)]
    for load in loads:
        load.start()

    loads[0].wait()
    loads[1].wait()
    high, low = split(x_ref[...])
    both = jnp.dot(jnp.concatenate([high, low, high], axis=1), phi_out[...], preferred_element_type=f32)
    wide_phi[:256, :] = both[:, :128]
    wide_phi[256:, :] = both[:, 128:]
    loads[2].wait()
    loads[3].wait()
    real = jnp.zeros((TP, PP), f32)
    imag = jnp.zeros((TP, PP), f32)

    def child(o, r):
        return jnp.concatenate([wide_phi[pl.ds(half * 256 + o * 32 + r, 16, stride=2), :] for half in range(2)], axis=0)

    for o in range(4):
        near = [child(o, r) for r in range(2)]
        far = [child(7 - o, r) for r in range(2)]
        high, low = split(jnp.concatenate(
            [near[0] + far[0], near[1] + far[1], near[0] - far[0], near[1] - far[1]], axis=1))
        wide = jnp.dot(theta_out[...], jnp.concatenate([high, low, high], axis=0), preferred_element_type=f32)
        cosine, sine = phases[o * 64:o * 64 + 64, :], phases[256 + o * 64:256 + o * 64 + 64, :]
        real += cosine * wide[:, :128] - sine * wide[:, 384:]
        imag += sine * wide[:, 256:384] + cosine * wide[:, 128:256]
    for i in range(NY):
        send0[i * 16:i * 16 + 8, :] = real[i * 8:i * 8 + 8]
        send0[i * 16 + 8:i * 16 + 16, :] = imag[i * 8:i * 8 + 8]

    pl.semaphore_wait(barrier, NY + NZ - 2 + 3)

    def along_y(source, landing, ssem, rsem, k, peer_slot):
        target = (y + k) % NY
        return pltpu.make_async_remote_copy(
            src_ref=source.at[pl.ds(pl.multiple_of(target * 16, 16), 16)],
            dst_ref=landing.at[pl.ds(pl.multiple_of(peer_slot * 16, 16), 16)],
            send_sem=ssem.at[k], recv_sem=rsem.at[k],
            device_id=(b, target * NZ + z), device_id_type=MESH)

    def along_z(source, landing, ssem, rsem, k, peer_slot):
        target = (z + k) % NZ
        return pltpu.make_async_remote_copy(
            src_ref=source.at[target], dst_ref=landing.at[peer_slot if peer_slot is not None else NEAR.index(-k % NZ)],
            send_sem=ssem.at[k], recv_sem=rsem.at[k],
            device_id=(b, y * NZ + target), device_id_type=MESH)

    for k in far_first:
        along_y(send0, recv1, ssem1, rsem1, k, y).start()
    mine = pl.ds(pl.multiple_of(y * 16, 16), 16)
    recv1[mine, :] = send0[mine, :]

    table_ref[2 * NTRANS:, :] = jnp.zeros((768 - 2 * NTRANS, 128), f32)
    for i in range(4, 7):
        loads[i].wait()
    for r in range(2):
        high, low = split(table_ref[pl.ds(r, 384, stride=2), :])
        tables[:384, r * 128:(r + 1) * 128] = high
        tables[384:, r * 128:(r + 1) * 128] = low
    diagonal = lax.broadcasted_iota(jnp.int32, (64, 64), 0) == lax.broadcasted_iota(jnp.int32, (64, 64), 1)
    count = jnp.broadcast_to(count_ref[...].astype(f32), (64, 64))
    count = jnp.sum(jnp.where(diagonal, count, 0.0), axis=1, keepdims=True)
    entry = lax.broadcasted_iota(jnp.int32, (64, NFAR), 1).astype(f32)
    by_chunk(trans_at, jnp.where(entry < count, (trans_ref[...] - 158).astype(f32), -256.0), -256.0)

    def gather_tables(first, until):
        def one(i, carry):
            columns = trans_at[pl.ds(pl.multiple_of(i * 8, 8), 8), :]
            gathered[pl.ds(pl.multiple_of(i * 512, 512), 512), :] = jnp.dot(
                one_hot(columns[:, :64], 158, 3), tables[...], preferred_element_type=f32)
            return carry
        lax.fori_loop(first, until, one, 0)

    gather_tables(0, 9)
    for k in range(1, NY):
        along_y(send0, recv1, ssem1, rsem1, k, (y + NY - k) % NY).wait_recv()
    for target in range(NZ):
        for r in range(2):
            send2[target, r] = recv1[pl.ds(r * 8 + target, 8, stride=16), :]
    for k in far_first:
        along_z(send2, pool.at[b], ssem2, rsem2, k, None).start()
    pool[b, 0] = send2[z]

    loads[7].wait()
    loads[8].wait()
    slot = slot_ref[...]
    chip = ((slot >> 6) - x) & 7
    chip = jnp.where(chip < 4, 2 * chip, 15 - 2 * chip)
    by_chunk(slot_at, (chip * 64 + (slot & 63) - 256).astype(f32), 0.0)
    chosen[...] = jnp.zeros((16, 128), f32)
    for g in range(GROUPS):
        chosen[g:g + 1, :CAP] = send_ref[g, pl.ds(b, 1), :].astype(f32)
    across_rows = chosen[...].T
    place = lax.broadcasted_iota(jnp.int32, (CAP, 64), 1)
    near = place >> 3
    near = jnp.where((near & 1) == 1, (near + 1) >> 1, 8 - (near >> 1))
    place = ((place & 7) * 8 + ((near + z) & 7)).astype(f32)
    for g in range(GROUPS):
        pick[g * CAP:(g + 1) * CAP, :64] = jnp.where(
            jnp.broadcast_to(across_rows[:CAP, g:g + 1], (CAP, 64)) == place, 1.0, 0.0).astype(BF)
    def from_origin(way, back):
        return (x + NX - back) % NX if way == 0 else (x + back) % NX

    def compact(way, back, parity):
        block = pool[from_origin(way, back) * 2 + parity]
        rank = 7 if back == 4 else 0 if back == 0 else 2 * back - 1 + way
        g = from_origin(way, back) * 2 + parity
        parts = [split(block[:, r].reshape(64, 128)) for r in range(2)]
        rows = pl.ds(pl.multiple_of(g * CAP, CAP), CAP)
        sent = jnp.dot(pick[rows, :64], jnp.concatenate([parts[0][0], parts[1][0], parts[0][1], parts[1][1]], axis=1),
                       preferred_element_type=f32).astype(BF)
        first = pl.multiple_of(rank // 4 * 512 + rank % 4 * 64 + parity * CAP, CAP)
        sources[pl.ds(first, CAP), :] = sent[:, :256]
        sources[pl.ds(pl.multiple_of(first + 256, CAP), CAP), :] = sent[:, 256:]

    slots = [(s, h) for s in range(3) for h in range(2)] + [(3, 0)]

    def ring(way, n, sent):
        s, h = slots[n]
        h = way if s == 3 else h
        block = pool.at[from_origin(way, s if sent else s + 1) * 2 + core, pl.ds(h * 4, 4)]
        return pltpu.make_async_remote_copy(
            src_ref=block, dst_ref=block, send_sem=ssem3.at[way, n], recv_sem=rsem3.at[way, n],
            device_id=((right, left)[way], d), device_id_type=MESH)

    def across(n, mine):
        if n == 0:
            back, way, part = 0, 0, pl.ds(0, 8)
        else:
            back, way = (n + 1) // 2, (n + 1) % 2
            part = pl.ds(0, 8) if back < 4 else pl.ds(way * 4, 4)
        block = pool.at[from_origin(way, back) * 2 + (core if mine else 1 - core), part]
        return pltpu.make_async_remote_copy(
            src_ref=block, dst_ref=block, send_sem=ssem4.at[n], recv_sem=rsem4.at[n],
            device_id=(other, d), device_id_type=MESH)

    def products(target, late):
        pieces = [one_hot(slot_at[pl.ds(pl.multiple_of(chunk * 64 + target * 8, 8), 8), :][:, :64], 0 if late else 256, 2)
                  for chunk in range(3)]
        field = jnp.dot(jnp.concatenate(pieces, axis=0), sources[late * 512:late * 512 + 512, :],
                        preferred_element_type=f32)
        real = jnp.zeros((8, 128), f32)
        imag = jnp.zeros((8, 128), f32)
        for chunk in range(3):
            weight = gathered[pl.ds(pl.multiple_of((chunk * 8 + target) * 512, 512), 512), :]
            rows = field[chunk * 512:chunk * 512 + 512]
            fr, fi, wr, wi = rows[:, :128], rows[:, 128:], weight[:, :128], weight[:, 128:]
            real += jnp.sum((fr * wr - fi * wi).reshape(64, 8, 128), axis=0)
            imag += jnp.sum((fr * wi + fi * wr).reshape(64, 8, 128), axis=0)
        return real, imag

    def early(first, until):
        def one(i, carry):
            real, imag = products(i, 0)
            halfway[pl.ds(pl.multiple_of(i * 16, 16), 8), :] = real
            halfway[pl.ds(pl.multiple_of(i * 16 + 8, 8), 8), :] = imag
            return carry
        lax.fori_loop(first, until, one, 0)

    gather_tables(9, 13)
    for half in range(2):
        for k in range(1, NZ):
            if NEAR.index(-k % NZ) // 4 == half:
                along_z(send2, pool.at[b], ssem2, rsem2, k, None).wait_recv()
        for way in range(2):
            ring(way, half, True).start()
        if half == 0:
            gather_tables(13, 16)
    across(0, True).start()
    compact(0, 0, core)
    unit = 16
    for n, (s, h) in enumerate(slots):
        for way in range(2):
            ring(way, n, False).wait_recv()
            if s < 2 or (s == 2 and h == way):
                ring(way, n + 2 if s < 2 else 6, True).start()
        if unit < 24:
            gather_tables(unit, unit + 2)
            unit += 2
        if h == 0 and s < 3:
            continue
        for way in range(2):
            across(2 * s + 1 + way, True).start()
        for way in range(2 if s < 3 else 1):
            compact(way, s + 1, core)
        for m in ((0,), (1, 2), (3, 4), (5, 6))[s]:
            across(m, False).wait_recv()
            way, back = (0, 0) if m == 0 else ((m + 1) % 2, (m + 1) // 2)
            compact(way, back, 1 - core)
        if s == 2:
            early(0, 5)
    early(5, 8)
    across(7, False).wait_recv()
    across(8, False).wait_recv()
    compact(0, 4, 1 - core)

    def one_owner(i, carry):
        k = 4 + (i + 1) // 2 * (1 - 2 * (i % 2))
        target = (y + k) % NY
        real, imag = products(target, 1)
        real += halfway[pl.ds(pl.multiple_of(target * 16, 16), 8), :]
        imag += halfway[pl.ds(pl.multiple_of(target * 16 + 8, 8), 8), :]
        back0[pl.ds(pl.multiple_of(target * 16, 16), 8), :] = real
        back0[pl.ds(pl.multiple_of(target * 16 + 8, 8), 8), :] = imag

        @pl.when(i < 7)
        def _():
            along_y(back0, back1, ssem5, rsem5, k, y).start()
        return carry

    lax.fori_loop(0, NY, one_owner, 0)
    back1[mine, :] = back0[mine, :]
    for load in loads[9:]:
        load.wait()
    for k in range(1, NY):
        along_y(back0, back1, ssem5, rsem5, k, (y + NY - k) % NY).wait_recv()
    for target in range(NZ):
        for r in range(2):
            back2[target, r] = back1[pl.ds(r * 8 + target, 8, stride=16), :]
    for k in far_first:
        along_z(back2, last, ssem6, rsem6, k, z).start()
    last[z] = back2[z]
    for k in range(1, NY):
        along_y(send0, recv1, ssem1, rsem1, k, y).wait_send()
        along_z(send2, pool.at[b], ssem2, rsem2, k, None).wait_send()
        along_y(back0, back1, ssem5, rsem5, k, y).wait_send()
    for n in range(7):
        for way in range(2):
            ring(way, n, True).wait_send()
    for n in range(9):
        across(n, True).wait_send()
    for k in range(1, NZ):
        along_z(back2, last, ssem6, rsem6, k, (z + NZ - k) % NZ).wait_recv()

    real = last[:, 0].reshape(TP, PP)
    imag = last[:, 1].reshape(TP, PP)
    narrow = [None] * 16
    for o in range(4):
        cosine, sine = [jnp.concatenate([phases[pl.ds(half * 256 + o * 64 + i, 8, stride=8), :] for i in range(NZ)], axis=0)
                        for half in range(2)]
        high, low = split(jnp.concatenate([cosine * real, sine * imag, cosine * imag, sine * real], axis=1))
        rows = jnp.dot(theta_in[...], jnp.concatenate([high, low, high], axis=0), preferred_element_type=f32)
        cr, si, ci, sr = [rows[:, i * 128:(i + 1) * 128] for i in range(4)]
        for n, value in ((o, cr + si), (7 - o, cr - si)):
            narrow[n * 2] = jnp.concatenate([value[:16], value[16:]], axis=1)
        for n, value in ((o, ci - sr), (7 - o, ci + sr)):
            narrow[n * 2 + 1] = jnp.concatenate([value[:16], value[16:]], axis=1)
    high, low = split(jnp.concatenate(narrow, axis=0))
    result = jnp.dot(jnp.concatenate([high, low, high], axis=1), phi_in[...], preferred_element_type=f32)
    for o in range(8):
        for r in range(2):
            n = o * 2 + r
            out_ref[pl.ds(o * 32 + r, 16, stride=2), :] = result[n * 16:(n + 1) * 16]
    for k in range(1, NZ):
        along_z(back2, last, ssem6, rsem6, k, z).wait_send()


def whole():
    return pl.BlockSpec(memory_space=pltpu.VMEM)


def dma(*shape):
    return pltpu.SemaphoreType.DMA(shape)


def whole_step(fields, table, send_rows, slots, trans, counts, const):
    f32, i32 = jnp.float32, jnp.int32
    vmem = pltpu.VMEM
    tile = (NZ, 2, NY, 128)
    return pl.pallas_call(
        kernel,
        out_shape=jax.ShapeDtypeStruct((256, 128), f32),
        in_specs=[pl.BlockSpec(memory_space=pl.ANY)] * 11, out_specs=whole(),
        scratch_shapes=[
            vmem((256, 128), f32), vmem((768, 128), f32), vmem((GROUPS, GROUPS, CAP), i32), vmem((64, NFAR), i32),
            vmem((64, NFAR), i32), vmem((1, 64), i32), vmem((384, 256), BF), vmem((64, 96), BF), vmem((512, 128), f32),
            vmem((32, 192), BF), vmem((768, 128), BF),
            vmem((512, 128), f32), vmem((128, 128), f32), vmem((128, 128), f32), vmem(tile, f32),
            vmem((GROUPS,) + tile, f32), vmem((192, 128), f32), vmem((192, 128), f32), vmem((16, 128), f32),
            vmem((GROUPS * CAP, 128), BF), vmem((2 * GROUPS * CAP, 256), BF), vmem((768, 256), BF),
            vmem((24 * 512, 256), f32),
            vmem((128, 128), f32), vmem((128, 128), f32), vmem((128, 128), f32), vmem(tile, f32), vmem(tile, f32), dma(11),
            dma(8), dma(8), dma(8), dma(8), dma(2, 7), dma(2, 7), dma(9), dma(9), dma(8), dma(8), dma(8), dma(8)],
        compiler_params=pltpu.CompilerParams(collective_id=0, has_side_effects=True, vmem_limit_bytes=60 << 20),
        name="level_pair",
    )(fields, table, send_rows, slots, trans, counts, *const)


def on_device(const, child_outgoing, trans_table, send_rows, far_slot, far_trans, far_count):
    fields = child_outgoing.reshape(8, 2, 16, 128).transpose(0, 2, 1, 3).reshape(256, 128)
    out = whole_step(fields, trans_table.reshape(NTRANS * 2, 128), send_rows, far_slot, far_trans,
                     far_count.reshape(1, 64), const)
    return out.reshape(8, 16, 2, 128).transpose(0, 2, 1, 3).reshape(8, 2, 2048)


def solution(mesh):
    placed = (
        P(("boxes", "dirs"), None, None),
        P(None, None, "dirs"),
        P(),
        P("boxes", None),
        P("boxes", None),
        P("boxes"),
    )
    const = constants()
    return jax.shard_map(
        functools.partial(on_device, const),
        mesh=mesh,
        in_specs=placed,
        out_specs=P(("boxes", "dirs"), None, None),
        check_vma=False,
    )
```

```python
import functools
import math

import jax
import jax.numpy as jnp
import numpy as np
from jax import lax
from jax.experimental import pallas as pl
from jax.experimental.pallas import tpu as pltpu
from jax.sharding import PartitionSpec as P

TC = 32
PC = 64
TP = 64
PP = 128
NTRANS = 316
NFAR = 189
CAP = 32
GROUPS = 16
SHIFT_PHASE = 2.7

NX = 8
NY = 8
NZ = 8
BF = jnp.bfloat16
MESH = pl.DeviceIdType.MESH
NEAR = (0, 1, 7, 2, 6, 3, 5, 4)


def interp_matrix(count_out, count_in, offset):
    target = (np.arange(count_out) + offset) / count_out
    source = (np.arange(count_in) + offset) / count_in
    spread = target[:, None] - source[None, :]
    orders = np.arange(1, count_in // 2)
    series = np.sum(np.cos(2.0 * math.pi * orders[None, None, :] * spread[:, :, None]), axis=2)
    return (1.0 + 2.0 * series + np.cos(math.pi * count_in * spread)) / count_in


def phase_tables():
    polar = math.pi * (np.arange(TP) + 0.5) / TP
    azimuth = 2.0 * math.pi * np.arange(PP) / PP
    wave_x = np.sin(polar)[:, None] * np.cos(azimuth)[None, :]
    wave_y = np.sin(polar)[:, None] * np.sin(azimuth)[None, :]
    wave_z = np.cos(polar)[:, None] * np.ones((1, PP))
    octant = np.arange(8)
    sign_x = (2 * (octant % 2) - 1)[:, None, None]
    sign_y = (2 * (octant // 2 % 2) - 1)[:, None, None]
    sign_z = (2 * (octant // 4) - 1)[:, None, None]
    angle = SHIFT_PHASE * (sign_x * wave_x + sign_y * wave_y + sign_z * wave_z)
    return np.cos(angle), np.sin(angle)


def halves(matrix):
    high = np.asarray(matrix, np.float32).astype(BF)
    low = (np.asarray(matrix, np.float32) - high.astype(np.float32)).astype(BF)
    return high, low


def constants():
    theta = interp_matrix(TP, TC, 0.5)
    phi = interp_matrix(PP, PC, 0.0)
    cosines, sines = phase_tables()
    pair = np.zeros((128, 256))
    pair[:64, :128] = phi.T
    pair[64:, 128:] = phi.T
    high, low = halves(pair)
    phi_out = np.concatenate([high, high, low], axis=0)
    theta_ba = np.concatenate([theta[:, 0::2], theta[:, 1::2]], axis=1)
    high, low = halves(theta_ba)
    theta_out = np.concatenate([high, high, low], axis=1)
    order = np.arange(64).reshape(8, 8).T.reshape(-1)
    high, low = halves(theta_ba.T[:, order])
    theta_in = np.concatenate([high, high, low], axis=1)
    back = np.zeros((256, 128))
    back[:128, :64] = phi
    back[128:, 64:] = phi
    high, low = halves(back * (TC * PC / (TP * PP)))
    phi_in = np.concatenate([high, high, low], axis=0)
    tables = np.concatenate([cosines[:4].reshape(256, 128), sines[:4].reshape(256, 128)]).astype(np.float32)
    return phi_out, theta_out, tables, theta_in, phi_in


def split(value):
    high = value.astype(BF)
    low = (value - high.astype(jnp.float32)).astype(BF)
    return high, low


def position():
    b = lax.axis_index("boxes")
    d = lax.axis_index("dirs")
    return b, b // 2, b % 2, d // NZ, d % NZ


def signal(barrier, device):
    pl.semaphore_signal(barrier, inc=1, device_id=device, device_id_type=MESH)


def one_hot(columns, first, tiles):
    lanes = lax.broadcasted_iota(jnp.int32, (16, 128), 1)
    numbers = [(lanes + (128 * k - first)).astype(jnp.float32).astype(BF) for k in range(tiles)]
    one, zero = jnp.ones((16, 128), BF), jnp.zeros((16, 128), BF)
    rows = []
    for e in range(0, 64, 2):
        column = jnp.concatenate([jnp.broadcast_to(columns[:, e + j:e + j + 1], (8, 128)) for j in range(2)], axis=0)
        column = column.astype(BF)
        rows.append([jnp.where(column == number, one, zero) for number in numbers])
    pieces = [jnp.concatenate([row[k] for row in rows], axis=0) for k in range(tiles)]
    return jnp.concatenate(pieces + pieces, axis=1)


def take(ref, sem):
    pltpu.make_async_copy(ref, ref, sem).wait()


def by_chunk(ref, lists, fill):
    for chunk in range(3):
        width = min(64, NFAR - chunk * 64)
        ref[chunk * 64:chunk * 64 + 64, :] = jnp.full((64, 128), fill, jnp.float32)
        ref[chunk * 64:chunk * 64 + 64, :width] = lists[:, chunk * 64:chunk * 64 + width]


def kernel(x_hbm, table_hbm, send_hbm, slot_hbm, trans_hbm, count_hbm, phi_out_hbm, theta_out_hbm, phases_hbm,
           theta_in_hbm, phi_in_hbm, out_ref,
           x_ref, table_ref, send_ref, slot_ref, trans_ref, count_ref, phi_out, theta_out, phases, theta_in, phi_in,
           wide_phi, send0, recv1, send2, pool, slot_at, trans_at, chosen, pick, sources, tables, gathered,
           halfway, back0, back1, back2, last, load_sem,
           ssem1, rsem1, ssem2, rsem2, ssem3, rsem3, ssem4, rsem4, ssem5, rsem5, ssem6, rsem6):
    f32 = jnp.float32
    b, x, core, y, z = position()
    d = y * NZ + z
    right = (x + 1) % NX * 2 + core
    left = (x + NX - 1) % NX * 2 + core
    other = x * 2 + 1 - core
    barrier = pltpu.get_barrier_semaphore()
    far_first = (4, 3, 5, 2, 6, 1, 7)
    for k in far_first:
        signal(barrier, (b, (y + k) % NY * NZ + z))
        signal(barrier, (b, y * NZ + (z + k) % NZ))
    for device in (right, left, other):
        signal(barrier, (device, d))
    pairs = [(x_hbm, x_ref), (phi_out_hbm, phi_out), (theta_out_hbm, theta_out), (phases_hbm, phases),
             (table_hbm, table_ref.at[pl.ds(0, 2 * NTRANS)]), (trans_hbm, trans_ref), (count_hbm, count_ref),
             (slot_hbm, slot_ref), (send_hbm, send_ref), (theta_in_hbm, theta_in), (phi_in_hbm, phi_in)]
    loads = [pltpu.make_async_copy(src, dst, load_sem.at[i]) for i, (src, dst) in enumerate(pairs)]
    for load in loads:
        load.start()

    loads[0].wait()
    loads[1].wait()
    high, low = split(x_ref[...])
    both = jnp.dot(jnp.concatenate([high, low, high], axis=1), phi_out[...], preferred_element_type=f32)
    wide_phi[:256, :] = both[:, :128]
    wide_phi[256:, :] = both[:, 128:]
    loads[2].wait()
    loads[3].wait()
    real = jnp.zeros((TP, PP), f32)
    imag = jnp.zeros((TP, PP), f32)

    def child(o, r):
        return jnp.concatenate([wide_phi[pl.ds(half * 256 + o * 32 + r, 16, stride=2), :] for half in range(2)], axis=0)

    for o in range(4):
        near = [child(o, r) for r in range(2)]
        far = [child(7 - o, r) for r in range(2)]
        high, low = split(jnp.concatenate(
            [near[0] + far[0], near[1] + far[1], near[0] - far[0], near[1] - far[1]], axis=1))
        wide = jnp.dot(theta_out[...], jnp.concatenate([high, low, high], axis=0), preferred_element_type=f32)
        cosine, sine = phases[o * 64:o * 64 + 64, :], phases[256 + o * 64:256 + o * 64 + 64, :]
        real += cosine * wide[:, :128] - sine * wide[:, 384:]
        imag += sine * wide[:, 256:384] + cosine * wide[:, 128:256]
    for i in range(NY):
        send0[i * 16:i * 16 + 8, :] = real[i * 8:i * 8 + 8]
        send0[i * 16 + 8:i * 16 + 16, :] = imag[i * 8:i * 8 + 8]

    pl.semaphore_wait(barrier, NY + NZ - 2 + 3)

    def along_y(source, landing, ssem, rsem, k, peer_slot):
        target = (y + k) % NY
        return pltpu.make_async_remote_copy(
            src_ref=source.at[pl.ds(pl.multiple_of(target * 16, 16), 16)],
            dst_ref=landing.at[pl.ds(pl.multiple_of(peer_slot * 16, 16), 16)],
            send_sem=ssem, recv_sem=rsem,
            device_id=(b, target * NZ + z), device_id_type=MESH)

    def along_z(source, landing, ssem, rsem, k, peer_slot):
        target = (z + k) % NZ
        return pltpu.make_async_remote_copy(
            src_ref=source.at[target], dst_ref=landing.at[peer_slot if peer_slot is not None else NEAR.index(-k % NZ)],
            send_sem=ssem, recv_sem=rsem,
            device_id=(b, y * NZ + target), device_id_type=MESH)

    for k in far_first:
        along_y(send0, recv1, ssem1, rsem1, k, y).start()
    mine = pl.ds(pl.multiple_of(y * 16, 16), 16)
    recv1[mine, :] = send0[mine, :]

    table_ref[2 * NTRANS:, :] = jnp.zeros((768 - 2 * NTRANS, 128), f32)
    for i in range(4, 7):
        loads[i].wait()
    for r in range(2):
        high, low = split(table_ref[pl.ds(r, 384, stride=2), :])
        tables[:384, r * 128:(r + 1) * 128] = high
        tables[384:, r * 128:(r + 1) * 128] = low
    diagonal = lax.broadcasted_iota(jnp.int32, (64, 64), 0) == lax.broadcasted_iota(jnp.int32, (64, 64), 1)
    count = jnp.broadcast_to(count_ref[...].astype(f32), (64, 64))
    count = jnp.sum(jnp.where(diagonal, count, 0.0), axis=1, keepdims=True)
    entry = lax.broadcasted_iota(jnp.int32, (64, NFAR), 1).astype(f32)
    by_chunk(trans_at, jnp.where(entry < count, (trans_ref[...] - 158).astype(f32), -256.0), -256.0)

    def gather_tables(first, until):
        def one(i, carry):
            columns = trans_at[pl.ds(pl.multiple_of(i * 8, 8), 8), :]
            gathered[pl.ds(pl.multiple_of(i * 512, 512), 512), :] = jnp.dot(
                one_hot(columns[:, :64], 158, 3), tables[...], preferred_element_type=f32)
            return carry
        lax.fori_loop(first, until, one, 0)

    gather_tables(0, 9)
    take(recv1.at[pl.ds(0, 112)], rsem1)
    for target in range(NZ):
        for r in range(2):
            send2[target, r] = recv1[pl.ds(r * 8 + target, 8, stride=16), :]
    for k in far_first:
        along_z(send2, pool.at[b], ssem2, rsem2, k, None).start()
    pool[b, 0] = send2[z]

    loads[7].wait()
    loads[8].wait()
    slot = slot_ref[...]
    chip = ((slot >> 6) - x) & 7
    chip = jnp.where(chip < 4, 2 * chip, 15 - 2 * chip)
    by_chunk(slot_at, (chip * 64 + (slot & 63) - 256).astype(f32), 0.0)
    chosen[...] = jnp.zeros((16, 128), f32)
    for g in range(GROUPS):
        chosen[g:g + 1, :CAP] = send_ref[g, pl.ds(b, 1), :].astype(f32)
    across_rows = chosen[...].T
    place = lax.broadcasted_iota(jnp.int32, (CAP, 64), 1)
    near = place >> 3
    near = jnp.where((near & 1) == 1, (near + 1) >> 1, 8 - (near >> 1))
    place = ((place & 7) * 8 + ((near + z) & 7)).astype(f32)
    for g in range(GROUPS):
        pick[g * CAP:(g + 1) * CAP, :64] = jnp.where(
            jnp.broadcast_to(across_rows[:CAP, g:g + 1], (CAP, 64)) == place, 1.0, 0.0).astype(BF)
    def from_origin(way, back):
        return (x + NX - back) % NX if way == 0 else (x + back) % NX

    def compact(way, back, parity):
        block = pool[from_origin(way, back) * 2 + parity]
        rank = 7 if back == 4 else 0 if back == 0 else 2 * back - 1 + way
        g = from_origin(way, back) * 2 + parity
        parts = [split(block[:, r].reshape(64, 128)) for r in range(2)]
        rows = pl.ds(pl.multiple_of(g * CAP, CAP), CAP)
        sent = jnp.dot(pick[rows, :64], jnp.concatenate([parts[0][0], parts[1][0], parts[0][1], parts[1][1]], axis=1),
                       preferred_element_type=f32).astype(BF)
        first = pl.multiple_of(rank // 4 * 512 + rank % 4 * 64 + parity * CAP, CAP)
        sources[pl.ds(first, CAP), :] = sent[:, :256]
        sources[pl.ds(pl.multiple_of(first + 256, CAP), CAP), :] = sent[:, 256:]

    def ring(way, s):
        block = pool.at[from_origin(way, s) * 2 + core]
        if s == 3:
            block = block.at[pl.ds(way * 4, 4)]
        return pltpu.make_async_remote_copy(
            src_ref=block, dst_ref=block, send_sem=ssem3, recv_sem=rsem3.at[s],
            device_id=((right, left)[way], d), device_id_type=MESH)

    def across(way, back):
        block = pool.at[from_origin(way, back) * 2 + core]
        return pltpu.make_async_remote_copy(
            src_ref=block, dst_ref=block, send_sem=ssem4, recv_sem=rsem4.at[back],
            device_id=(other, d), device_id_type=MESH)

    def products(target, late):
        pieces = [one_hot(slot_at[pl.ds(pl.multiple_of(chunk * 64 + target * 8, 8), 8), :][:, :64], 0 if late else 256, 2)
                  for chunk in range(3)]
        field = jnp.dot(jnp.concatenate(pieces, axis=0), sources[late * 512:late * 512 + 512, :],
                        preferred_element_type=f32)
        real = jnp.zeros((8, 128), f32)
        imag = jnp.zeros((8, 128), f32)
        for chunk in range(3):
            weight = gathered[pl.ds(pl.multiple_of((chunk * 8 + target) * 512, 512), 512), :]
            rows = field[chunk * 512:chunk * 512 + 512]
            fr, fi, wr, wi = rows[:, :128], rows[:, 128:], weight[:, :128], weight[:, 128:]
            real += jnp.sum((fr * wr - fi * wi).reshape(64, 8, 128), axis=0)
            imag += jnp.sum((fr * wi + fi * wr).reshape(64, 8, 128), axis=0)
        return real, imag

    def early(first, until):
        def one(i, carry):
            real, imag = products(i, 0)
            halfway[pl.ds(pl.multiple_of(i * 16, 16), 8), :] = real
            halfway[pl.ds(pl.multiple_of(i * 16 + 8, 8), 8), :] = imag
            return carry
        lax.fori_loop(first, until, one, 0)

    gather_tables(9, 16)
    take(pool.at[b, pl.ds(1, 7)], rsem2)
    for way in range(2):
        ring(way, 0).start()
    across(0, 0).start()
    compact(0, 0, core)
    gather_tables(16, 18)
    for s in range(4):
        take(pool.at[pl.ds(0, 2)] if s < 3 else pool.at[0], rsem3.at[s])
        for way in range(2):
            if s < 3:
                ring(way, s + 1).start()
        for way in range(2 if s < 3 else 1):
            across(way, s + 1).start()
        for way in range(2 if s < 3 else 1):
            compact(way, s + 1, core)
        if s < 2:
            gather_tables(18 + 3 * s, 21 + 3 * s)
        if s == 3:
            early(4, 8)
        take(pool.at[pl.ds(0, 2)] if s > 0 else pool.at[0], rsem4.at[s])
        for way in range(2 if s > 0 else 1):
            compact(way, s, 1 - core)
        if s == 2:
            early(0, 4)
    take(pool.at[0], rsem4.at[4])
    compact(0, 4, 1 - core)

    def one_owner(i, carry):
        k = 4 + (i + 1) // 2 * (1 - 2 * (i % 2))
        target = (y + k) % NY
        real, imag = products(target, 1)
        real += halfway[pl.ds(pl.multiple_of(target * 16, 16), 8), :]
        imag += halfway[pl.ds(pl.multiple_of(target * 16 + 8, 8), 8), :]
        back0[pl.ds(pl.multiple_of(target * 16, 16), 8), :] = real
        back0[pl.ds(pl.multiple_of(target * 16 + 8, 8), 8), :] = imag

        @pl.when(i < 7)
        def _():
            along_y(back0, back1, ssem5, rsem5, k, y).start()
        return carry

    lax.fori_loop(0, NY, one_owner, 0)
    back1[mine, :] = back0[mine, :]
    for load in loads[9:]:
        load.wait()
    take(back1.at[pl.ds(0, 112)], rsem5)
    for target in range(NZ):
        for r in range(2):
            back2[target, r] = back1[pl.ds(r * 8 + target, 8, stride=16), :]
    for k in far_first:
        along_z(back2, last, ssem6, rsem6, k, z).start()
    last[z] = back2[z]
    take(send0.at[pl.ds(0, 112)], ssem1)
    take(send2.at[pl.ds(0, 7)], ssem2)
    take(pool.at[pl.ds(0, 7)], ssem3)
    take(pool.at[pl.ds(0, 8)], ssem4)
    take(back0.at[pl.ds(0, 112)], ssem5)
    take(last.at[pl.ds(0, 7)], rsem6)

    real = last[:, 0].reshape(TP, PP)
    imag = last[:, 1].reshape(TP, PP)
    narrow = [None] * 16
    for o in range(4):
        cosine, sine = [jnp.concatenate([phases[pl.ds(half * 256 + o * 64 + i, 8, stride=8), :] for i in range(NZ)], axis=0)
                        for half in range(2)]
        high, low = split(jnp.concatenate([cosine * real, sine * imag, cosine * imag, sine * real], axis=1))
        rows = jnp.dot(theta_in[...], jnp.concatenate([high, low, high], axis=0), preferred_element_type=f32)
        cr, si, ci, sr = [rows[:, i * 128:(i + 1) * 128] for i in range(4)]
        for n, value in ((o, cr + si), (7 - o, cr - si)):
            narrow[n * 2] = jnp.concatenate([value[:16], value[16:]], axis=1)
        for n, value in ((o, ci - sr), (7 - o, ci + sr)):
            narrow[n * 2 + 1] = jnp.concatenate([value[:16], value[16:]], axis=1)
    high, low = split(jnp.concatenate(narrow, axis=0))
    result = jnp.dot(jnp.concatenate([high, low, high], axis=1), phi_in[...], preferred_element_type=f32)
    for o in range(8):
        for r in range(2):
            n = o * 2 + r
            out_ref[pl.ds(o * 32 + r, 16, stride=2), :] = result[n * 16:(n + 1) * 16]
    take(back2.at[pl.ds(0, 7)], ssem6)


def whole():
    return pl.BlockSpec(memory_space=pltpu.VMEM)


def dma(*shape):
    return pltpu.SemaphoreType.DMA(shape)


def whole_step(fields, table, send_rows, slots, trans, counts, const):
    f32, i32 = jnp.float32, jnp.int32
    vmem = pltpu.VMEM
    tile = (NZ, 2, NY, 128)
    return pl.pallas_call(
        kernel,
        out_shape=jax.ShapeDtypeStruct((256, 128), f32),
        in_specs=[pl.BlockSpec(memory_space=pl.ANY)] * 11, out_specs=whole(),
        scratch_shapes=[
            vmem((256, 128), f32), vmem((768, 128), f32), vmem((GROUPS, GROUPS, CAP), i32), vmem((64, NFAR), i32),
            vmem((64, NFAR), i32), vmem((1, 64), i32), vmem((384, 256), BF), vmem((64, 96), BF), vmem((512, 128), f32),
            vmem((32, 192), BF), vmem((768, 128), BF),
            vmem((512, 128), f32), vmem((128, 128), f32), vmem((128, 128), f32), vmem(tile, f32),
            vmem((GROUPS,) + tile, f32), vmem((192, 128), f32), vmem((192, 128), f32), vmem((16, 128), f32),
            vmem((GROUPS * CAP, 128), BF), vmem((2 * GROUPS * CAP, 256), BF), vmem((768, 256), BF),
            vmem((24 * 512, 256), f32),
            vmem((128, 128), f32), vmem((128, 128), f32), vmem((128, 128), f32), vmem(tile, f32), vmem(tile, f32), dma(11),
            dma(), dma(), dma(), dma(), dma(), dma(4), dma(), dma(5), dma(), dma(), dma(), dma()],
        compiler_params=pltpu.CompilerParams(collective_id=0, has_side_effects=True, vmem_limit_bytes=60 << 20),
        name="level_pair",
    )(fields, table, send_rows, slots, trans, counts, *const)


def on_device(const, child_outgoing, trans_table, send_rows, far_slot, far_trans, far_count):
    fields = child_outgoing.reshape(8, 2, 16, 128).transpose(0, 2, 1, 3).reshape(256, 128)
    out = whole_step(fields, trans_table.reshape(NTRANS * 2, 128), send_rows, far_slot, far_trans,
                     far_count.reshape(1, 64), const)
    return out.reshape(8, 16, 2, 128).transpose(0, 2, 1, 3).reshape(8, 2, 2048)


def solution(mesh):
    placed = (
        P(("boxes", "dirs"), None, None),
        P(None, None, "dirs"),
        P(),
        P("boxes", None),
        P("boxes", None),
        P("boxes"),
    )
    const = constants()
    return jax.shard_map(
        functools.partial(on_device, const),
        mesh=mesh,
        in_specs=placed,
        out_specs=P(("boxes", "dirs"), None, None),
        check_vma=False,
    )
```

```python
import functools
import math

import jax
import jax.numpy as jnp
import numpy as np
from jax import lax
from jax.experimental import pallas as pl
from jax.experimental.pallas import tpu as pltpu
from jax.sharding import PartitionSpec as P

TC = 32
PC = 64
TP = 64
PP = 128
NTRANS = 316
NFAR = 189
CAP = 32
GROUPS = 16
SHIFT_PHASE = 2.7

NX = 8
NY = 8
NZ = 8
BF = jnp.bfloat16
MESH = pl.DeviceIdType.MESH
NEAR = (0, 1, 7, 2, 6, 3, 5, 4)


def interp_matrix(count_out, count_in, offset):
    target = (np.arange(count_out) + offset) / count_out
    source = (np.arange(count_in) + offset) / count_in
    spread = target[:, None] - source[None, :]
    orders = np.arange(1, count_in // 2)
    series = np.sum(np.cos(2.0 * math.pi * orders[None, None, :] * spread[:, :, None]), axis=2)
    return (1.0 + 2.0 * series + np.cos(math.pi * count_in * spread)) / count_in


def phase_tables():
    polar = math.pi * (np.arange(TP) + 0.5) / TP
    azimuth = 2.0 * math.pi * np.arange(PP) / PP
    wave_x = np.sin(polar)[:, None] * np.cos(azimuth)[None, :]
    wave_y = np.sin(polar)[:, None] * np.sin(azimuth)[None, :]
    wave_z = np.cos(polar)[:, None] * np.ones((1, PP))
    octant = np.arange(8)
    sign_x = (2 * (octant % 2) - 1)[:, None, None]
    sign_y = (2 * (octant // 2 % 2) - 1)[:, None, None]
    sign_z = (2 * (octant // 4) - 1)[:, None, None]
    angle = SHIFT_PHASE * (sign_x * wave_x + sign_y * wave_y + sign_z * wave_z)
    return np.cos(angle), np.sin(angle)


def halves(matrix):
    high = np.asarray(matrix, np.float32).astype(BF)
    low = (np.asarray(matrix, np.float32) - high.astype(np.float32)).astype(BF)
    return high, low


def constants():
    theta = interp_matrix(TP, TC, 0.5)
    phi = interp_matrix(PP, PC, 0.0)
    cosines, sines = phase_tables()
    pair = np.zeros((128, 256))
    pair[:64, :128] = phi.T
    pair[64:, 128:] = phi.T
    high, low = halves(pair)
    phi_out = np.concatenate([high, high, low], axis=0)
    theta_ba = np.concatenate([theta[:, 0::2], theta[:, 1::2]], axis=1)
    high, low = halves(theta_ba)
    theta_out = np.concatenate([high, high, low], axis=1)
    order = np.arange(64).reshape(8, 8).T.reshape(-1)
    high, low = halves(theta_ba.T[:, order])
    theta_in = np.concatenate([high, high, low], axis=1)
    back = np.zeros((256, 128))
    back[:128, :64] = phi
    back[128:, 64:] = phi
    high, low = halves(back * (TC * PC / (TP * PP)))
    phi_in = np.concatenate([high, high, low], axis=0)
    tables = np.concatenate([cosines[:4].reshape(256, 128), sines[:4].reshape(256, 128)]).astype(np.float32)
    return phi_out, theta_out, tables, theta_in, phi_in


def split(value):
    high = value.astype(BF)
    low = (value - high.astype(jnp.float32)).astype(BF)
    return high, low


def position():
    b = lax.axis_index("boxes")
    d = lax.axis_index("dirs")
    return b, b // 2, b % 2, d // NZ, d % NZ


def signal(barrier, device):
    pl.semaphore_signal(barrier, inc=1, device_id=device, device_id_type=MESH)


def one_hot(columns, first, tiles):
    lanes = lax.broadcasted_iota(jnp.int32, (16, 128), 1)
    numbers = [(lanes + (128 * k - first)).astype(jnp.float32).astype(BF) for k in range(tiles)]
    one, zero = jnp.ones((16, 128), BF), jnp.zeros((16, 128), BF)
    rows = []
    for e in range(0, 64, 2):
        column = jnp.concatenate([jnp.broadcast_to(columns[:, e + j:e + j + 1], (8, 128)) for j in range(2)], axis=0)
        column = column.astype(BF)
        rows.append([jnp.where(column == number, one, zero) for number in numbers])
    pieces = [jnp.concatenate([row[k] for row in rows], axis=0) for k in range(tiles)]
    return jnp.concatenate(pieces + pieces, axis=1)


def take(ref, sem):
    pltpu.make_async_copy(ref, ref, sem).wait()


def by_chunk(ref, lists, fill):
    for chunk in range(3):
        width = min(64, NFAR - chunk * 64)
        ref[chunk * 64:chunk * 64 + 64, :] = jnp.full((64, 128), fill, jnp.float32)
        ref[chunk * 64:chunk * 64 + 64, :width] = lists[:, chunk * 64:chunk * 64 + width]


def kernel(x_hbm, table_hbm, send_hbm, slot_hbm, trans_hbm, count_hbm, phi_out_hbm, theta_out_hbm, phases_hbm,
           theta_in_hbm, phi_in_hbm, out_ref,
           x_ref, table_ref, send_ref, slot_ref, trans_ref, count_ref, phi_out, theta_out, phases, theta_in, phi_in,
           wide_phi, send0, recv1, send2, pool, slot_at, trans_at, chosen, pick, sources, tables, gathered,
           halfway, back0, back1, back2, last, load_sem,
           ssem1, rsem1, ssem2, rsem2, ssem3, rsem3, ssem4, rsem4, ssem5, rsem5, ssem6, rsem6):
    f32 = jnp.float32
    b, x, core, y, z = position()
    d = y * NZ + z
    right = (x + 1) % NX * 2 + core
    left = (x + NX - 1) % NX * 2 + core
    other = x * 2 + 1 - core
    barrier = pltpu.get_barrier_semaphore()
    far_first = (4, 3, 5, 2, 6, 1, 7)
    for k in far_first:
        signal(barrier, (b, (y + k) % NY * NZ + z))
        signal(barrier, (b, y * NZ + (z + k) % NZ))
    for device in (right, left, other):
        signal(barrier, (device, d))
    pairs = [(x_hbm, x_ref), (phi_out_hbm, phi_out), (theta_out_hbm, theta_out), (phases_hbm, phases),
             (table_hbm, table_ref.at[pl.ds(0, 2 * NTRANS)]), (trans_hbm, trans_ref), (count_hbm, count_ref),
             (slot_hbm, slot_ref), (send_hbm, send_ref), (theta_in_hbm, theta_in), (phi_in_hbm, phi_in)]
    loads = [pltpu.make_async_copy(src, dst, load_sem.at[i]) for i, (src, dst) in enumerate(pairs)]
    for load in loads:
        load.start()

    loads[0].wait()
    loads[1].wait()
    high, low = split(x_ref[...])
    both = jnp.dot(jnp.concatenate([high, low, high], axis=1), phi_out[...], preferred_element_type=f32)
    wide_phi[:256, :] = both[:, :128]
    wide_phi[256:, :] = both[:, 128:]
    loads[2].wait()
    loads[3].wait()
    real = jnp.zeros((TP, PP), f32)
    imag = jnp.zeros((TP, PP), f32)

    def child(o, r):
        return jnp.concatenate([wide_phi[pl.ds(half * 256 + o * 32 + r, 16, stride=2), :] for half in range(2)], axis=0)

    for o in range(4):
        near = [child(o, r) for r in range(2)]
        far = [child(7 - o, r) for r in range(2)]
        high, low = split(jnp.concatenate(
            [near[0] + far[0], near[1] + far[1], near[0] - far[0], near[1] - far[1]], axis=1))
        wide = jnp.dot(theta_out[...], jnp.concatenate([high, low, high], axis=0), preferred_element_type=f32)
        cosine, sine = phases[o * 64:o * 64 + 64, :], phases[256 + o * 64:256 + o * 64 + 64, :]
        real += cosine * wide[:, :128] - sine * wide[:, 384:]
        imag += sine * wide[:, 256:384] + cosine * wide[:, 128:256]
    for i in range(NY):
        send0[i * 16:i * 16 + 8, :] = real[i * 8:i * 8 + 8]
        send0[i * 16 + 8:i * 16 + 16, :] = imag[i * 8:i * 8 + 8]

    pl.semaphore_wait(barrier, NY + NZ - 2 + 3)

    def along_y(source, landing, ssem, rsem, k, peer_slot):
        target = (y + k) % NY
        return pltpu.make_async_remote_copy(
            src_ref=source.at[pl.ds(pl.multiple_of(target * 16, 16), 16)],
            dst_ref=landing.at[pl.ds(pl.multiple_of(peer_slot * 16, 16), 16)],
            send_sem=ssem, recv_sem=rsem,
            device_id=(b, target * NZ + z), device_id_type=MESH)

    def along_z(source, landing, ssem, rsem, k, peer_slot):
        target = (z + k) % NZ
        return pltpu.make_async_remote_copy(
            src_ref=source.at[target], dst_ref=landing.at[peer_slot if peer_slot is not None else NEAR.index(-k % NZ)],
            send_sem=ssem, recv_sem=rsem,
            device_id=(b, y * NZ + target), device_id_type=MESH)

    for k in far_first:
        along_y(send0, recv1, ssem1, rsem1, k, y).start()
    mine = pl.ds(pl.multiple_of(y * 16, 16), 16)
    recv1[mine, :] = send0[mine, :]

    table_ref[2 * NTRANS:, :] = jnp.zeros((768 - 2 * NTRANS, 128), f32)
    for i in range(4, 7):
        loads[i].wait()
    for r in range(2):
        high, low = split(table_ref[pl.ds(r, 384, stride=2), :])
        tables[:384, r * 128:(r + 1) * 128] = high
        tables[384:, r * 128:(r + 1) * 128] = low
    diagonal = lax.broadcasted_iota(jnp.int32, (64, 64), 0) == lax.broadcasted_iota(jnp.int32, (64, 64), 1)
    count = jnp.broadcast_to(count_ref[...].astype(f32), (64, 64))
    count = jnp.sum(jnp.where(diagonal, count, 0.0), axis=1, keepdims=True)
    entry = lax.broadcasted_iota(jnp.int32, (64, NFAR), 1).astype(f32)
    by_chunk(trans_at, jnp.where(entry < count, (trans_ref[...] - 158).astype(f32), -256.0), -256.0)

    def gather_tables(first, until):
        def one(i, carry):
            columns = trans_at[pl.ds(pl.multiple_of(i * 8, 8), 8), :]
            gathered[pl.ds(pl.multiple_of(i * 512, 512), 512), :] = jnp.dot(
                one_hot(columns[:, :64], 158, 3), tables[...], preferred_element_type=f32)
            return carry
        lax.fori_loop(first, until, one, 0)

    gather_tables(0, 12)
    take(recv1.at[pl.ds(0, 112)], rsem1)
    for target in range(NZ):
        for r in range(2):
            send2[target, r] = recv1[pl.ds(r * 8 + target, 8, stride=16), :]
    for k in far_first:
        along_z(send2, pool.at[b], ssem2, rsem2, k, None).start()
    pool[b, 0] = send2[z]

    loads[7].wait()
    loads[8].wait()
    slot = slot_ref[...]
    chip = ((slot >> 6) - x) & 7
    chip = jnp.where(chip < 4, 2 * chip, 15 - 2 * chip)
    by_chunk(slot_at, (chip * 64 + (slot & 63) - 256).astype(f32), 0.0)
    chosen[...] = jnp.zeros((16, 128), f32)
    for g in range(GROUPS):
        chosen[g:g + 1, :CAP] = send_ref[g, pl.ds(b, 1), :].astype(f32)
    across_rows = chosen[...].T
    place = lax.broadcasted_iota(jnp.int32, (CAP, 64), 1)
    near = place >> 3
    near = jnp.where((near & 1) == 1, (near + 1) >> 1, 8 - (near >> 1))
    place = ((place & 7) * 8 + ((near + z) & 7)).astype(f32)
    for g in range(GROUPS):
        pick[g * CAP:(g + 1) * CAP, :64] = jnp.where(
            jnp.broadcast_to(across_rows[:CAP, g:g + 1], (CAP, 64)) == place, 1.0, 0.0).astype(BF)
    def from_origin(way, back):
        return (x + NX - back) % NX if way == 0 else (x + back) % NX

    def compact(way, back, parity):
        block = pool[from_origin(way, back) * 2 + parity]
        rank = 7 if back == 4 else 0 if back == 0 else 2 * back - 1 + way
        g = from_origin(way, back) * 2 + parity
        parts = [split(block[:, r].reshape(64, 128)) for r in range(2)]
        rows = pl.ds(pl.multiple_of(g * CAP, CAP), CAP)
        sent = jnp.dot(pick[rows, :64], jnp.concatenate([parts[0][0], parts[1][0], parts[0][1], parts[1][1]], axis=1),
                       preferred_element_type=f32).astype(BF)
        first = pl.multiple_of(rank // 4 * 512 + rank % 4 * 64 + parity * CAP, CAP)
        sources[pl.ds(first, CAP), :] = sent[:, :256]
        sources[pl.ds(pl.multiple_of(first + 256, CAP), CAP), :] = sent[:, 256:]

    def ring(way, s):
        block = pool.at[from_origin(way, s) * 2 + core]
        if s == 3:
            block = block.at[pl.ds(way * 4, 4)]
        return pltpu.make_async_remote_copy(
            src_ref=block, dst_ref=block, send_sem=ssem3, recv_sem=rsem3.at[s],
            device_id=((right, left)[way], d), device_id_type=MESH)

    def across(way, back):
        block = pool.at[from_origin(way, back) * 2 + core]
        return pltpu.make_async_remote_copy(
            src_ref=block, dst_ref=block, send_sem=ssem4, recv_sem=rsem4.at[back],
            device_id=(other, d), device_id_type=MESH)

    def products(target, late):
        pieces = [one_hot(slot_at[pl.ds(pl.multiple_of(chunk * 64 + target * 8, 8), 8), :][:, :64], 0 if late else 256, 2)
                  for chunk in range(3)]
        field = jnp.dot(jnp.concatenate(pieces, axis=0), sources[late * 512:late * 512 + 512, :],
                        preferred_element_type=f32)
        real = jnp.zeros((8, 128), f32)
        imag = jnp.zeros((8, 128), f32)
        for chunk in range(3):
            weight = gathered[pl.ds(pl.multiple_of((chunk * 8 + target) * 512, 512), 512), :]
            rows = field[chunk * 512:chunk * 512 + 512]
            fr, fi, wr, wi = rows[:, :128], rows[:, 128:], weight[:, :128], weight[:, 128:]
            real += jnp.sum((fr * wr - fi * wi).reshape(64, 8, 128), axis=0)
            imag += jnp.sum((fr * wi + fi * wr).reshape(64, 8, 128), axis=0)
        return real, imag

    def early(first, until):
        def one(i, carry):
            real, imag = products(i, 0)
            halfway[pl.ds(pl.multiple_of(i * 16, 16), 8), :] = real
            halfway[pl.ds(pl.multiple_of(i * 16 + 8, 8), 8), :] = imag
            return carry
        lax.fori_loop(first, until, one, 0)

    gather_tables(12, 22)
    take(pool.at[b, pl.ds(1, 7)], rsem2)
    for way in range(2):
        ring(way, 0).start()
    across(0, 0).start()
    compact(0, 0, core)
    gather_tables(22, 24)
    for s in range(4):
        take(pool.at[pl.ds(0, 2)] if s < 3 else pool.at[0], rsem3.at[s])
        for way in range(2):
            if s < 3:
                ring(way, s + 1).start()
        for way in range(2 if s < 3 else 1):
            across(way, s + 1).start()
        for way in range(2 if s < 3 else 1):
            compact(way, s + 1, core)
        if s == 0:
            take(pool.at[0], rsem4.at[0])
            compact(0, 0, 1 - core)
        if s > 1:
            early(3 * s - 4, 3 * s - 1)
        take(pool.at[pl.ds(0, 2)] if s < 3 else pool.at[0], rsem4.at[s + 1])
        for way in range(2 if s < 3 else 1):
            compact(way, s + 1, 1 - core)
        if s == 1:
            early(0, 2)

    def one_owner(i, carry):
        k = 4 + (i + 1) // 2 * (1 - 2 * (i % 2))
        target = (y + k) % NY
        real, imag = products(target, 1)
        real += halfway[pl.ds(pl.multiple_of(target * 16, 16), 8), :]
        imag += halfway[pl.ds(pl.multiple_of(target * 16 + 8, 8), 8), :]
        back0[pl.ds(pl.multiple_of(target * 16, 16), 8), :] = real
        back0[pl.ds(pl.multiple_of(target * 16 + 8, 8), 8), :] = imag

        @pl.when(i < 7)
        def _():
            along_y(back0, back1, ssem5, rsem5, k, y).start()
        return carry

    lax.fori_loop(0, NY, one_owner, 0)
    back1[mine, :] = back0[mine, :]
    for load in loads[9:]:
        load.wait()
    take(back1.at[pl.ds(0, 112)], rsem5)
    for target in range(NZ):
        for r in range(2):
            back2[target, r] = back1[pl.ds(r * 8 + target, 8, stride=16), :]
    for k in far_first:
        along_z(back2, last, ssem6, rsem6, k, z).start()
    last[z] = back2[z]
    take(send0.at[pl.ds(0, 112)], ssem1)
    take(send2.at[pl.ds(0, 7)], ssem2)
    take(pool.at[pl.ds(0, 7)], ssem3)
    take(pool.at[pl.ds(0, 8)], ssem4)
    take(back0.at[pl.ds(0, 112)], ssem5)
    take(last.at[pl.ds(0, 7)], rsem6)

    real = last[:, 0].reshape(TP, PP)
    imag = last[:, 1].reshape(TP, PP)
    narrow = [None] * 16
    for o in range(4):
        cosine, sine = [jnp.concatenate([phases[pl.ds(half * 256 + o * 64 + i, 8, stride=8), :] for i in range(NZ)], axis=0)
                        for half in range(2)]
        high, low = split(jnp.concatenate([cosine * real, sine * imag, cosine * imag, sine * real], axis=1))
        rows = jnp.dot(theta_in[...], jnp.concatenate([high, low, high], axis=0), preferred_element_type=f32)
        cr, si, ci, sr = [rows[:, i * 128:(i + 1) * 128] for i in range(4)]
        for n, value in ((o, cr + si), (7 - o, cr - si)):
            narrow[n * 2] = jnp.concatenate([value[:16], value[16:]], axis=1)
        for n, value in ((o, ci - sr), (7 - o, ci + sr)):
            narrow[n * 2 + 1] = jnp.concatenate([value[:16], value[16:]], axis=1)
    high, low = split(jnp.concatenate(narrow, axis=0))
    result = jnp.dot(jnp.concatenate([high, low, high], axis=1), phi_in[...], preferred_element_type=f32)
    for o in range(8):
        for r in range(2):
            n = o * 2 + r
            out_ref[pl.ds(o * 32 + r, 16, stride=2), :] = result[n * 16:(n + 1) * 16]
    take(back2.at[pl.ds(0, 7)], ssem6)


def whole():
    return pl.BlockSpec(memory_space=pltpu.VMEM)


def dma(*shape):
    return pltpu.SemaphoreType.DMA(shape)


def whole_step(fields, table, send_rows, slots, trans, counts, const):
    f32, i32 = jnp.float32, jnp.int32
    vmem = pltpu.VMEM
    tile = (NZ, 2, NY, 128)
    return pl.pallas_call(
        kernel,
        out_shape=jax.ShapeDtypeStruct((256, 128), f32),
        in_specs=[pl.BlockSpec(memory_space=pl.ANY)] * 11, out_specs=whole(),
        scratch_shapes=[
            vmem((256, 128), f32), vmem((768, 128), f32), vmem((GROUPS, GROUPS, CAP), i32), vmem((64, NFAR), i32),
            vmem((64, NFAR), i32), vmem((1, 64), i32), vmem((384, 256), BF), vmem((64, 96), BF), vmem((512, 128), f32),
            vmem((32, 192), BF), vmem((768, 128), BF),
            vmem((512, 128), f32), vmem((128, 128), f32), vmem((128, 128), f32), vmem(tile, f32),
            vmem((GROUPS,) + tile, f32), vmem((192, 128), f32), vmem((192, 128), f32), vmem((16, 128), f32),
            vmem((GROUPS * CAP, 128), BF), vmem((2 * GROUPS * CAP, 256), BF), vmem((768, 256), BF),
            vmem((24 * 512, 256), f32),
            vmem((128, 128), f32), vmem((128, 128), f32), vmem((128, 128), f32), vmem(tile, f32), vmem(tile, f32), dma(11),
            dma(), dma(), dma(), dma(), dma(), dma(4), dma(), dma(5), dma(), dma(), dma(), dma()],
        compiler_params=pltpu.CompilerParams(collective_id=0, has_side_effects=True, vmem_limit_bytes=60 << 20),
        name="level_pair",
    )(fields, table, send_rows, slots, trans, counts, *const)


def on_device(const, child_outgoing, trans_table, send_rows, far_slot, far_trans, far_count):
    fields = child_outgoing.reshape(8, 2, 16, 128).transpose(0, 2, 1, 3).reshape(256, 128)
    out = whole_step(fields, trans_table.reshape(NTRANS * 2, 128), send_rows, far_slot, far_trans,
                     far_count.reshape(1, 64), const)
    return out.reshape(8, 16, 2, 128).transpose(0, 2, 1, 3).reshape(8, 2, 2048)


def solution(mesh):
    placed = (
        P(("boxes", "dirs"), None, None),
        P(None, None, "dirs"),
        P(),
        P("boxes", None),
        P("boxes", None),
        P("boxes"),
    )
    const = constants()
    return jax.shard_map(
        functools.partial(on_device, const),
        mesh=mesh,
        in_specs=placed,
        out_specs=P(("boxes", "dirs"), None, None),
        check_vma=False,
    )
```

```python
import functools
import math

import jax
import jax.numpy as jnp
import numpy as np
from jax import lax
from jax.experimental import pallas as pl
from jax.experimental.pallas import tpu as pltpu
from jax.sharding import PartitionSpec as P

TC = 32
PC = 64
TP = 64
PP = 128
NTRANS = 316
NFAR = 189
CAP = 32
GROUPS = 16
SHIFT_PHASE = 2.7

NX = 8
NY = 8
NZ = 8
BF = jnp.bfloat16
MESH = pl.DeviceIdType.MESH
NEAR = (0, 1, 7, 2, 6, 3, 5, 4)


def interp_matrix(count_out, count_in, offset):
    target = (np.arange(count_out) + offset) / count_out
    source = (np.arange(count_in) + offset) / count_in
    spread = target[:, None] - source[None, :]
    orders = np.arange(1, count_in // 2)
    series = np.sum(np.cos(2.0 * math.pi * orders[None, None, :] * spread[:, :, None]), axis=2)
    return (1.0 + 2.0 * series + np.cos(math.pi * count_in * spread)) / count_in


def phase_tables():
    polar = math.pi * (np.arange(TP) + 0.5) / TP
    azimuth = 2.0 * math.pi * np.arange(PP) / PP
    wave_x = np.sin(polar)[:, None] * np.cos(azimuth)[None, :]
    wave_y = np.sin(polar)[:, None] * np.sin(azimuth)[None, :]
    wave_z = np.cos(polar)[:, None] * np.ones((1, PP))
    octant = np.arange(8)
    sign_x = (2 * (octant % 2) - 1)[:, None, None]
    sign_y = (2 * (octant // 2 % 2) - 1)[:, None, None]
    sign_z = (2 * (octant // 4) - 1)[:, None, None]
    angle = SHIFT_PHASE * (sign_x * wave_x + sign_y * wave_y + sign_z * wave_z)
    return np.cos(angle), np.sin(angle)


def halves(matrix):
    high = np.asarray(matrix, np.float32).astype(BF)
    low = (np.asarray(matrix, np.float32) - high.astype(np.float32)).astype(BF)
    return high, low


def constants():
    theta = interp_matrix(TP, TC, 0.5)
    phi = interp_matrix(PP, PC, 0.0)
    cosines, sines = phase_tables()
    pair = np.zeros((128, 256))
    pair[:64, :128] = phi.T
    pair[64:, 128:] = phi.T
    high, low = halves(pair)
    phi_out = np.concatenate([high, high, low], axis=0)
    theta_ba = np.concatenate([theta[:, 0::2], theta[:, 1::2]], axis=1)
    high, low = halves(theta_ba)
    theta_out = np.concatenate([high, high, low], axis=1)
    order = np.arange(64).reshape(8, 8).T.reshape(-1)
    high, low = halves(theta_ba.T[:, order])
    theta_in = np.concatenate([high, high, low], axis=1)
    back = np.zeros((256, 128))
    back[:128, :64] = phi
    back[128:, 64:] = phi
    high, low = halves(back)
    phi_in = np.concatenate([high, high, low], axis=0)
    tables = np.concatenate([cosines[:4].reshape(256, 128), sines[:4].reshape(256, 128)]).astype(np.float32)
    return phi_out, theta_out, tables, theta_in, phi_in


def split(value):
    high = value.astype(BF)
    low = (value - high.astype(jnp.float32)).astype(BF)
    return high, low


def position():
    b = lax.axis_index("boxes")
    d = lax.axis_index("dirs")
    return b, b // 2, b % 2, d // NZ, d % NZ


def signal(barrier, device):
    pl.semaphore_signal(barrier, inc=1, device_id=device, device_id_type=MESH)


def one_hot(columns, first, tiles):
    lanes = lax.broadcasted_iota(jnp.int32, (16, 128), 1)
    numbers = [(lanes + (128 * k - first)).astype(jnp.float32).astype(BF) for k in range(tiles)]
    one, zero = jnp.ones((16, 128), BF), jnp.zeros((16, 128), BF)
    rows = []
    for e in range(0, 64, 2):
        column = jnp.concatenate([jnp.broadcast_to(columns[:, e + j:e + j + 1], (8, 128)) for j in range(2)], axis=0)
        column = column.astype(BF)
        rows.append([jnp.where(column == number, one, zero) for number in numbers])
    pieces = [jnp.concatenate([row[k] for row in rows], axis=0) for k in range(tiles)]
    return jnp.concatenate(pieces + pieces, axis=1)


def take(ref, sem):
    pltpu.make_async_copy(ref, ref, sem).wait()


def by_chunk(ref, lists, fill):
    for chunk in range(3):
        width = min(64, NFAR - chunk * 64)
        ref[chunk * 64:chunk * 64 + 64, :] = jnp.full((64, 128), fill, jnp.float32)
        ref[chunk * 64:chunk * 64 + 64, :width] = lists[:, chunk * 64:chunk * 64 + width]


def kernel(x_hbm, table_hbm, send_hbm, slot_hbm, trans_hbm, count_hbm, phi_out_hbm, theta_out_hbm, phases_hbm,
           theta_in_hbm, phi_in_hbm, out_ref,
           x_ref, table_ref, send_ref, slot_ref, trans_ref, count_ref, phi_out, theta_out, phases, theta_in, phi_in,
           wide_phi, send0, recv1, send2, pool, slot_at, trans_at, chosen, pick, sources, tables, gathered,
           halfway, back0, back1, back2, last, load_sem,
           ssem1, rsem1, ssem2, rsem2, ssem3, rsem3, ssem4, rsem4, ssem5, rsem5, ssem6, rsem6):
    f32 = jnp.float32
    b, x, core, y, z = position()
    d = y * NZ + z
    right = (x + 1) % NX * 2 + core
    left = (x + NX - 1) % NX * 2 + core
    other = x * 2 + 1 - core
    barrier = pltpu.get_barrier_semaphore()
    far_first = (4, 3, 5, 2, 6, 1, 7)
    for k in far_first:
        signal(barrier, (b, (y + k) % NY * NZ + z))
        signal(barrier, (b, y * NZ + (z + k) % NZ))
    for device in (right, left, other):
        signal(barrier, (device, d))
    pairs = [(x_hbm, x_ref), (phi_out_hbm, phi_out), (theta_out_hbm, theta_out), (phases_hbm, phases),
             (table_hbm, table_ref.at[pl.ds(0, 2 * NTRANS)]), (trans_hbm, trans_ref), (count_hbm, count_ref),
             (slot_hbm, slot_ref), (send_hbm, send_ref), (theta_in_hbm, theta_in), (phi_in_hbm, phi_in)]
    loads = [pltpu.make_async_copy(src, dst, load_sem.at[i]) for i, (src, dst) in enumerate(pairs)]
    for load in loads:
        load.start()

    loads[0].wait()
    loads[1].wait()
    high, low = split(x_ref[...])
    both = jnp.dot(jnp.concatenate([high, low, high], axis=1), phi_out[...], preferred_element_type=f32)
    wide_phi[:256, :] = both[:, :128]
    wide_phi[256:, :] = both[:, 128:]
    loads[2].wait()
    loads[3].wait()
    real = jnp.zeros((TP, PP), f32)
    imag = jnp.zeros((TP, PP), f32)

    def child(o, r):
        return jnp.concatenate([wide_phi[pl.ds(half * 256 + o * 32 + r, 16, stride=2), :] for half in range(2)], axis=0)

    for o in range(4):
        near = [child(o, r) for r in range(2)]
        far = [child(7 - o, r) for r in range(2)]
        high, low = split(jnp.concatenate(
            [near[0] + far[0], near[1] + far[1], near[0] - far[0], near[1] - far[1]], axis=1))
        wide = jnp.dot(theta_out[...], jnp.concatenate([high, low, high], axis=0), preferred_element_type=f32)
        cosine, sine = phases[o * 64:o * 64 + 64, :], phases[256 + o * 64:256 + o * 64 + 64, :]
        real += cosine * wide[:, :128] - sine * wide[:, 384:]
        imag += sine * wide[:, 256:384] + cosine * wide[:, 128:256]
    for i in range(NY):
        send0[i * 16:i * 16 + 8, :] = real[i * 8:i * 8 + 8]
        send0[i * 16 + 8:i * 16 + 16, :] = imag[i * 8:i * 8 + 8]

    pl.semaphore_wait(barrier, NY + NZ - 2 + 3)

    def along_y(source, landing, ssem, rsem, k, peer_slot):
        target = (y + k) % NY
        return pltpu.make_async_remote_copy(
            src_ref=source.at[pl.ds(pl.multiple_of(target * 16, 16), 16)],
            dst_ref=landing.at[pl.ds(pl.multiple_of(peer_slot * 16, 16), 16)],
            send_sem=ssem, recv_sem=rsem,
            device_id=(b, target * NZ + z), device_id_type=MESH)

    def along_z(source, landing, ssem, rsem, k, peer_slot):
        target = (z + k) % NZ
        return pltpu.make_async_remote_copy(
            src_ref=source.at[target], dst_ref=landing.at[peer_slot if peer_slot is not None else NEAR.index(-k % NZ)],
            send_sem=ssem, recv_sem=rsem,
            device_id=(b, y * NZ + target), device_id_type=MESH)

    for k in far_first:
        along_y(send0, recv1, ssem1, rsem1, k, y).start()
    mine = pl.ds(pl.multiple_of(y * 16, 16), 16)
    recv1[mine, :] = send0[mine, :]

    table_ref[2 * NTRANS:, :] = jnp.zeros((768 - 2 * NTRANS, 128), f32)
    for i in range(4, 7):
        loads[i].wait()
    for r in range(2):
        high, low = split(table_ref[pl.ds(r, 384, stride=2), :])
        tables[:384, r * 128:(r + 1) * 128] = high
        tables[384:, r * 128:(r + 1) * 128] = low
    diagonal = lax.broadcasted_iota(jnp.int32, (64, 64), 0) == lax.broadcasted_iota(jnp.int32, (64, 64), 1)
    count = jnp.broadcast_to(count_ref[...].astype(f32), (64, 64))
    count = jnp.sum(jnp.where(diagonal, count, 0.0), axis=1, keepdims=True)
    entry = lax.broadcasted_iota(jnp.int32, (64, NFAR), 1).astype(f32)
    by_chunk(trans_at, jnp.where(entry < count, (trans_ref[...] - 158).astype(f32), -256.0), -256.0)

    def gather_tables(first, until):
        def one(i, carry):
            columns = trans_at[pl.ds(pl.multiple_of(i * 8, 8), 8), :]
            gathered[pl.ds(pl.multiple_of(i * 512, 512), 512), :] = jnp.dot(
                one_hot(columns[:, :64], 158, 3), tables[...], preferred_element_type=f32)
            return carry
        lax.fori_loop(first, until, one, 0)

    gather_tables(0, 12)
    take(recv1.at[pl.ds(0, 112)], rsem1)
    for target in range(NZ):
        for r in range(2):
            send2[target, r] = recv1[pl.ds(r * 8 + target, 8, stride=16), :]
    for k in far_first:
        along_z(send2, pool.at[b], ssem2, rsem2, k, None).start()
    pool[b, 0] = send2[z]

    loads[7].wait()
    loads[8].wait()
    slot = slot_ref[...]
    chip = ((slot >> 6) - x) & 7
    chip = jnp.where(chip < 4, 2 * chip, 15 - 2 * chip)
    by_chunk(slot_at, (chip * 64 + (slot & 63) - 256).astype(f32), 0.0)
    chosen[...] = jnp.zeros((16, 128), f32)
    for g in range(GROUPS):
        chosen[g:g + 1, :CAP] = send_ref[g, pl.ds(b, 1), :].astype(f32)
    across_rows = chosen[...].T
    place = lax.broadcasted_iota(jnp.int32, (CAP, 64), 1)
    near = place >> 3
    near = jnp.where((near & 1) == 1, (near + 1) >> 1, 8 - (near >> 1))
    place = ((place & 7) * 8 + ((near + z) & 7)).astype(f32)
    for g in range(GROUPS):
        pick[g * CAP:(g + 1) * CAP, :64] = jnp.where(
            jnp.broadcast_to(across_rows[:CAP, g:g + 1], (CAP, 64)) == place, 1.0, 0.0).astype(BF)
    def from_origin(way, back):
        return (x + NX - back) % NX if way == 0 else (x + back) % NX

    def compact(way, back, parity):
        block = pool[from_origin(way, back) * 2 + parity]
        rank = 7 if back == 4 else 0 if back == 0 else 2 * back - 1 + way
        g = from_origin(way, back) * 2 + parity
        parts = [split(block[:, r].reshape(64, 128)) for r in range(2)]
        rows = pl.ds(pl.multiple_of(g * CAP, CAP), CAP)
        sent = jnp.dot(pick[rows, :64], jnp.concatenate([parts[0][0], parts[1][0], parts[0][1], parts[1][1]], axis=1),
                       preferred_element_type=f32).astype(BF)
        first = pl.multiple_of(rank // 4 * 512 + rank % 4 * 64 + parity * CAP, CAP)
        sources[pl.ds(first, CAP), :] = sent[:, :256]
        sources[pl.ds(pl.multiple_of(first + 256, CAP), CAP), :] = sent[:, 256:]

    def ring(way, s):
        block = pool.at[from_origin(way, s) * 2 + core]
        if s == 3:
            block = block.at[pl.ds(way * 4, 4)]
        return pltpu.make_async_remote_copy(
            src_ref=block, dst_ref=block, send_sem=ssem3, recv_sem=rsem3.at[s],
            device_id=((right, left)[way], d), device_id_type=MESH)

    def across(way, back):
        block = pool.at[from_origin(way, back) * 2 + core]
        return pltpu.make_async_remote_copy(
            src_ref=block, dst_ref=block, send_sem=ssem4, recv_sem=rsem4.at[back],
            device_id=(other, d), device_id_type=MESH)

    def products(target, late):
        pieces = [one_hot(slot_at[pl.ds(pl.multiple_of(chunk * 64 + target * 8, 8), 8), :][:, :64], 0 if late else 256, 2)
                  for chunk in range(3)]
        field = jnp.dot(jnp.concatenate(pieces, axis=0), sources[late * 512:late * 512 + 512, :],
                        preferred_element_type=f32)
        real = jnp.zeros((8, 128), f32)
        imag = jnp.zeros((8, 128), f32)
        for chunk in range(3):
            weight = gathered[pl.ds(pl.multiple_of((chunk * 8 + target) * 512, 512), 512), :]
            rows = field[chunk * 512:chunk * 512 + 512]
            fr, fi, wr, wi = rows[:, :128], rows[:, 128:], weight[:, :128], weight[:, 128:]
            real += jnp.sum((fr * wr - fi * wi).reshape(64, 8, 128), axis=0)
            imag += jnp.sum((fr * wi + fi * wr).reshape(64, 8, 128), axis=0)
        return real, imag

    def early(first, until):
        def one(i, carry):
            real, imag = products(i, 0)
            halfway[pl.ds(pl.multiple_of(i * 16, 16), 8), :] = real
            halfway[pl.ds(pl.multiple_of(i * 16 + 8, 8), 8), :] = imag
            return carry
        lax.fori_loop(first, until, one, 0)

    gather_tables(12, 22)
    take(pool.at[b, pl.ds(1, 7)], rsem2)
    for way in range(2):
        ring(way, 0).start()
    across(0, 0).start()
    compact(0, 0, core)
    gather_tables(22, 24)
    for s in range(4):
        take(pool.at[pl.ds(0, 2)] if s < 3 else pool.at[0], rsem3.at[s])
        for way in range(2):
            if s < 3:
                ring(way, s + 1).start()
        for way in range(2 if s < 3 else 1):
            across(way, s + 1).start()
        for way in range(2 if s < 3 else 1):
            compact(way, s + 1, core)
        if s == 0:
            take(pool.at[0], rsem4.at[0])
            compact(0, 0, 1 - core)
        if s > 1:
            early(3 if s == 2 else 7, 7 if s == 2 else 8)
        take(pool.at[pl.ds(0, 2)] if s < 3 else pool.at[0], rsem4.at[s + 1])
        for way in range(2 if s < 3 else 1):
            compact(way, s + 1, 1 - core)
        if s == 1:
            early(0, 3)

    def one_owner(i, carry):
        k = 4 + (i + 1) // 2 * (1 - 2 * (i % 2))
        target = (y + k) % NY
        real, imag = products(target, 1)
        real += halfway[pl.ds(pl.multiple_of(target * 16, 16), 8), :]
        imag += halfway[pl.ds(pl.multiple_of(target * 16 + 8, 8), 8), :]
        back0[pl.ds(pl.multiple_of(target * 16, 16), 8), :] = real
        back0[pl.ds(pl.multiple_of(target * 16 + 8, 8), 8), :] = imag

        @pl.when(i < 7)
        def _():
            along_y(back0, back1, ssem5, rsem5, k, y).start()
        return carry

    lax.fori_loop(0, NY, one_owner, 0)
    back1[mine, :] = back0[mine, :]
    for load in loads[9:]:
        load.wait()
    take(back1.at[pl.ds(0, 112)], rsem5)
    for target in range(NZ):
        for r in range(2):
            back2[target, r] = back1[pl.ds(r * 8 + target, 8, stride=16), :]
    for k in far_first:
        along_z(back2, last, ssem6, rsem6, k, z).start()
    last[z] = back2[z]
    take(send0.at[pl.ds(0, 112)], ssem1)
    take(send2.at[pl.ds(0, 7)], ssem2)
    take(pool.at[pl.ds(0, 7)], ssem3)
    take(pool.at[pl.ds(0, 8)], ssem4)
    take(back0.at[pl.ds(0, 112)], ssem5)
    take(last.at[pl.ds(0, 7)], rsem6)

    real = last[:, 0].reshape(TP, PP)
    imag = last[:, 1].reshape(TP, PP)
    narrow = [None] * 16
    for o in range(4):
        cosine, sine = [jnp.concatenate([phases[pl.ds(half * 256 + o * 64 + i, 8, stride=8), :] for i in range(NZ)], axis=0)
                        for half in range(2)]
        high, low = split(jnp.concatenate([cosine * real, sine * imag, cosine * imag, sine * real], axis=1))
        rows = jnp.dot(theta_in[...], jnp.concatenate([high, low, high], axis=0), preferred_element_type=f32)
        cr, si, ci, sr = [rows[:, i * 128:(i + 1) * 128] for i in range(4)]
        for n, value in ((o, cr + si), (7 - o, cr - si)):
            narrow[n * 2] = jnp.concatenate([value[:16], value[16:]], axis=1)
        for n, value in ((o, ci - sr), (7 - o, ci + sr)):
            narrow[n * 2 + 1] = jnp.concatenate([value[:16], value[16:]], axis=1)
    high, low = split(jnp.concatenate(narrow, axis=0))
    result = jnp.dot(jnp.concatenate([high, low, high], axis=1), phi_in[...], preferred_element_type=f32)
    for o in range(8):
        for r in range(2):
            n = o * 2 + r
            out_ref[pl.ds(o * 32 + r, 16, stride=2), :] = result[n * 16:(n + 1) * 16]
    take(back2.at[pl.ds(0, 7)], ssem6)


def whole():
    return pl.BlockSpec(memory_space=pltpu.VMEM)


def dma(*shape):
    return pltpu.SemaphoreType.DMA(shape)


def whole_step(fields, table, send_rows, slots, trans, counts, const):
    f32, i32 = jnp.float32, jnp.int32
    vmem = pltpu.VMEM
    tile = (NZ, 2, NY, 128)
    return pl.pallas_call(
        kernel,
        out_shape=jax.ShapeDtypeStruct((256, 128), f32),
        in_specs=[pl.BlockSpec(memory_space=pl.ANY)] * 11, out_specs=whole(),
        scratch_shapes=[
            vmem((256, 128), f32), vmem((768, 128), f32), vmem((GROUPS, GROUPS, CAP), i32), vmem((64, NFAR), i32),
            vmem((64, NFAR), i32), vmem((1, 64), i32), vmem((384, 256), BF), vmem((64, 96), BF), vmem((512, 128), f32),
            vmem((32, 192), BF), vmem((768, 128), BF),
            vmem((512, 128), f32), vmem((128, 128), f32), vmem((128, 128), f32), vmem(tile, f32),
            vmem((GROUPS,) + tile, f32), vmem((192, 128), f32), vmem((192, 128), f32), vmem((16, 128), f32),
            vmem((GROUPS * CAP, 128), BF), vmem((2 * GROUPS * CAP, 256), BF), vmem((768, 256), BF),
            vmem((24 * 512, 256), f32),
            vmem((128, 128), f32), vmem((128, 128), f32), vmem((128, 128), f32), vmem(tile, f32), vmem(tile, f32), dma(11),
            dma(), dma(), dma(), dma(), dma(), dma(4), dma(), dma(5), dma(), dma(), dma(), dma()],
        compiler_params=pltpu.CompilerParams(collective_id=0, has_side_effects=True, vmem_limit_bytes=60 << 20),
        name="level_pair",
    )(fields, table, send_rows, slots, trans, counts, *const)


def on_device(const, child_outgoing, trans_table, send_rows, far_slot, far_trans, far_count):
    fields = child_outgoing.reshape(8, 2, 16, 128).transpose(0, 2, 1, 3).reshape(256, 128)
    out = whole_step(fields, trans_table.reshape(NTRANS * 2, 128), send_rows, far_slot, far_trans,
                     far_count.reshape(1, 64), const)
    return out.reshape(8, 16, 2, 128).transpose(0, 2, 1, 3).reshape(8, 2, 2048) * (TC * PC / (TP * PP))


def solution(mesh):
    placed = (
        P(("boxes", "dirs"), None, None),
        P(None, None, "dirs"),
        P(),
        P("boxes", None),
        P("boxes", None),
        P("boxes"),
    )
    const = constants()
    return jax.shard_map(
        functools.partial(on_device, const),
        mesh=mesh,
        in_specs=placed,
        out_specs=P(("boxes", "dirs"), None, None),
        check_vma=False,
    )
```
